32 devices in a mesh: row: 8 (over z, y), col: 4 (over x, core).
Axes of the slice: x: 2, y: 2, z: 4, core: 2. Of those that a mesh axis runs over, the one named last changes fastest.
Arguments:
- weights: float32 [192, 16, 64, 64], P('row', 'col'), may hold values from 9.765625e-05 to 0.0029296875
- block_cols: int32 [192, 16], P('row'), may hold values from 0 to 191, as said below
- counts: int32 [192], P('row'), may hold values from 1 to 16, as said below
- near_null: float32 [192, 64], P('row'), may hold values from 0.5 to 2
- prior_ridge: float32 [192, 64], P('row'), may hold values from 0.1 to 1
Outputs:
- coarse_band: float32 [192, 128], P(('row', 'col'))
The draws below stay inside these ranges and needn't reach their ends.
Inputs may be any that keep to these rules, and one draw needn't show every extreme that they name: `block_cols`: row i holds i in slot 0; its other slots hold distinct aggregates j with (j - i) modulo 192 between -21 and 21 and not 0; some row holds a neighbour at +21 and some at -21. Slots at or beyond a row's count are unused. `counts`: both ends are reached in every draw; the mean over the 24 rows of one index of row differs from index to index.
All inputs are finite; a program needn't handle non-finite values.
Results may differ from the reference program's by a relative error of at most 0.0003.
Values sent between devices are 32-bit elements; how exact they have to be, the bound alone decides.
No kernel may reach another device: no remote copies, remote signals or barrier semaphores. Data moves between devices by JAX's collectives and lax.ppermute only.
A program may use at most 64 MiB of HBM per device.

```python
import math
import jax
import jax.numpy as jnp
from jax import lax

B = 64
KA = 16
H = 21
BAND = 128
BR = 24
NBLK = 192


def draw_block_cols(key, part):
    span = 2 * H
    candidates = jnp.arange(span, dtype=jnp.int32)
    values = jnp.where(candidates < H, candidates - H, candidates - H + 1)
    key_one, key_two, key_three = jax.random.split(key, 3)
    scores = jax.random.randint(key_one, (NBLK, span), 0, 1 << 20, dtype=jnp.int32) * span + candidates[None, :]
    row_up = jax.random.randint(key_two, (), 0, NBLK, dtype=jnp.int32)
    row_down = jax.random.randint(key_three, (), 0, NBLK, dtype=jnp.int32)
    scores = scores.at[row_up, span - 1].set(-1)
    scores = scores.at[row_down, 0].set(-2)
    order = jnp.argsort(scores, axis=1)[:, :KA - 1]
    chosen = values[order]
    offsets = jnp.concatenate([jnp.zeros((NBLK, 1), jnp.int32), chosen], axis=1)
    return ((jnp.arange(NBLK, dtype=jnp.int32)[:, None] + offsets) % NBLK).astype(jnp.int32)


def draw_counts(key, part):
    key_one, key_two, key_three, key_four = jax.random.split(key, 4)
    levels = jax.random.randint(key_one, (NBLK // BR,), 1, 5, dtype=jnp.int32)
    base_draw = jax.random.randint(key_two, (NBLK,), 0, KA, dtype=jnp.int32)
    result = 1 + base_draw * jnp.repeat(levels, BR) // 4
    top_row = jax.random.randint(key_three, (), 0, NBLK, dtype=jnp.int32)
    low_row = (top_row + 1 + jax.random.randint(key_four, (), 0, NBLK - 1, dtype=jnp.int32)) % NBLK
    result = result.at[top_row].set(KA).at[low_row].set(1)
    return result.astype(jnp.int32)


def level_of(key, shape, cuts, smallest, top_value):
    gain, own = 1.0, jax.random.fold_in(key, 6)
    for dim, blocks in cuts:
        draws = jnp.exp(jax.random.uniform(jax.random.fold_in(own, dim), (blocks,), jnp.float32, smallest / len(cuts), top_value / len(cuts)))
        gain = gain * jnp.repeat(draws, shape[dim] // blocks).reshape([-1 if axis == dim else 1 for axis in range(len(shape))])
    return gain


def setup_inputs(seed: int = 0) -> dict:
    key_list = jax.random.split(jax.random.key(seed), 6)
    weights = jnp.clip(jnp.exp(math.log(0.0029296875) - 3.4011974 * jax.random.uniform(key_list[0], (NBLK, KA, B, B), jnp.float32) ** level_of(key_list[0], (NBLK, KA, B, B), ((0, 8), (1, 4)), -0.2, 0.2)), 9.765625145519152e-05, 0.0029296875)
    block_cols = draw_block_cols(jax.random.fold_in(key_list[5], 71), 0)
    counts = draw_counts(jax.random.fold_in(key_list[5], 71), 0)
    near_null = jnp.clip(jnp.exp(math.log(2.0) - 1.3862944 * jax.random.uniform(key_list[3], (NBLK, B), jnp.float32) ** level_of(key_list[3], (NBLK, B), ((0, 8),), -0.2, 0.2)), 0.5, 2.0)
    prior_ridge = jnp.clip(jnp.exp(math.log(1.0) - 2.3025851 * jax.random.uniform(key_list[4], (NBLK, B), jnp.float32) ** level_of(key_list[4], (NBLK, B), ((0, 8),), -0.2, 0.2)), 0.1, 1.0)
    return dict(weights=weights, block_cols=block_cols, counts=counts, near_null=near_null, prior_ridge=prior_ridge)


epsilon = 1e-06
relax_weight = 2.0 / 3.0

def band_form(tiles, tile_offsets):
    one_hot = (tile_offsets[..., None] + BAND // 2 == jnp.arange(BAND, dtype=jnp.int32)[None, None, :]).astype(jnp.float32)
    return jnp.einsum('nkx,nkq->nxq', tiles, one_hot, precision=lax.Precision.HIGHEST)

def reference(weights, block_cols, counts, near_null, prior_ridge):
    highest = lax.Precision.HIGHEST
    rows_all = jnp.arange(NBLK, dtype=jnp.int32)
    offsets = (block_cols - rows_all[:, None] + H) % NBLK - H
    slot_ids = jnp.arange(KA, dtype=jnp.int32)
    mask_all = (slot_ids[None, :] < counts[:, None]).astype(jnp.float32)
    groups = NBLK // 4
    w_groups = weights.reshape(groups, 4, KA, B, B)
    m_groups = mask_all.reshape(groups, 4, KA)
    degree = lax.map(lambda pair: jnp.einsum('ikxy,ik->ix', pair[0], pair[1], precision=highest), (w_groups, m_groups))
    degree = degree.reshape(NBLK, B) + prior_ridge
    unit_null = near_null / jnp.sqrt(lax.optimization_barrier(jnp.sum(near_null * near_null, axis=1, keepdims=True)) + epsilon)
    near_rows = unit_null[block_cols]
    applied = lax.map(lambda pair: jnp.einsum('ikxy,iky->ikx', pair[0], pair[1], precision=highest), (w_groups, near_rows.reshape(groups, 4, KA, B)))
    applied = applied.reshape(NBLK, KA, B)
    own_term = jnp.where(slot_ids == 0, 1.0 - relax_weight, 0.0).astype(jnp.float32)[None, :, None] * unit_null[:, None, :]
    prolong = mask_all[:, :, None] * (own_term + relax_weight * applied / degree[:, None, :])
    band = band_form(prolong, offsets)
    band_pos = jnp.arange(BAND, dtype=jnp.int32)

    def one_group(pieces):
        tiles, cols, offs, mask, probe, degs, own_band = pieces
        picked = band[cols]
        source = (band_pos[None, None, :] - offs[:, :, None]) % BAND
        rolled = jnp.take_along_axis(picked, jnp.broadcast_to(source[:, :, None, :], picked.shape), axis=3)
        products = jnp.einsum('ikxy,ikyq->ikxq', tiles, rolled, precision=highest)
        applied_p = degs[:, :, None] * own_band - lax.optimization_barrier(jnp.sum(mask[:, :, None, None] * products, axis=1))
        contrib = jnp.einsum('ikx,ixq->ikq', probe, applied_p, precision=highest)
        back_index = (band_pos[None, None, :] + offs[:, :, None]) % BAND
        return jnp.take_along_axis(contrib, back_index, axis=2)
    shifted = lax.map(one_group, (w_groups, block_cols.reshape(groups, 4, KA), offsets.reshape(groups, 4, KA), m_groups, prolong.reshape(groups, 4, KA, B), degree.reshape(groups, 4, B), band.reshape(groups, 4, B, BAND)))
    shifted = shifted.reshape(NBLK * KA, BAND)
    return jax.ops.segment_sum(shifted, block_cols.reshape(-1), num_segments=NBLK)
```

```python
import functools

import jax
import jax.numpy as jnp
from jax import lax
from jax.experimental import pallas as pl
from jax.experimental.pallas import tpu as pltpu
from jax.sharding import PartitionSpec as P

H = 21
BAND = 128
LANES = 128

epsilon = 1e-06
relax_weight = 2.0 / 3.0

NT = (((1,), (1,)), ((), ()))
NN = (((1,), (0,)), ((), ()))
TN = (((0,), (0,)), ((), ()))


def mxu(a, b, dims):
    return lax.dot_general(a, b, dims, preferred_element_type=jnp.float32)


def split(x):
    hi = x.astype(jnp.bfloat16)
    lo = (x - hi.astype(jnp.float32)).astype(jnp.bfloat16)
    return hi, lo


def lane_iota(shape):
    return lax.broadcasted_iota(jnp.int32, shape, len(shape) - 1)


def row_iota(shape):
    return lax.broadcasted_iota(jnp.int32, shape, 0)


def pack_kernel(scal, counts, w_ref, hi_ref, lo_ref):
    rows, slots, size, _ = w_ref.shape
    start = scal[0] * slots
    per = LANES // size
    for i in range(rows):
        for p in range(slots // per):
            tile = jnp.concatenate([w_ref[i, per * p + h] for h in range(per)], axis=1)
            slot = lane_iota((size, LANES)) // size + (start + per * p)
            tile = jnp.where(slot < counts[i], tile, 0.0)
            hi, lo = split(tile)
            hi_ref[i, :, p * LANES : (p + 1) * LANES] = hi
            lo_ref[i, :, p * LANES : (p + 1) * LANES] = lo


def unit_kernel(size, scal, offs, counts, prev_ref, own_ref, next_ref, ridge_ref, hi_ref, lo_ref,
                block_ref, unit_ref, acc_ref):
    rows = own_ref.shape[0]
    slots = hi_ref.shape[2] // size
    column = scal[0]
    lane = lane_iota((rows, LANES))
    for g, ref in enumerate((prev_ref, own_ref, next_ref)):
        x = jnp.where(lane < size, ref[...], 0.0)
        unit = x / jnp.sqrt(jnp.sum(x * x, axis=1, keepdims=True) + epsilon)
        unit_ref[g * rows : (g + 1) * rows, :] = unit + pltpu.roll(unit, size, 1)
    row8 = row_iota((8, LANES))
    half = lane_iota((8, LANES)) // size
    for i in range(rows):
        parts = []
        for p in range(slots // 2):
            tile = jnp.where(row8 == slots, 1.0, 0.0)
            for h in range(2):
                k = 2 * p + h
                t = rows + i + offs[i, column * slots + k]
                vec = jnp.broadcast_to(unit_ref[pl.ds(t, 1), :], (8, LANES))
                tile = jnp.where((row8 == k) & (half == h), vec, tile)
            parts.append(tile)
        lhs = jnp.concatenate(parts, axis=1)
        hi, lo = split(lhs)
        both = mxu(jnp.concatenate([hi, lo], axis=0), hi_ref[i], NT)
        low = mxu(hi, lo_ref[i], NT)
        acc_ref[8 * i : 8 * i + 8, :] = both[:8] + both[8:] + low
    plane = [acc_ref[pl.ds(k, rows, stride=8), :] for k in range(slots + 1)]
    for p in range(slots // 2):
        block_ref[p * rows : (p + 1) * rows, :] = jnp.concatenate(plane[2 * p : 2 * p + 2], axis=1)
    degree = plane[slots] + jnp.where(column == 0, ridge_ref[...], 0.0)
    block_ref[(slots // 2) * rows :, :] = jnp.concatenate([degree, jnp.zeros_like(degree)], axis=1)


def hot_kernel(size, slots, ncol, scal, prev_ref, own_ref, next_ref, hot_ref, tmp_ref):
    rows = own_ref.shape[0]
    column = scal[0]
    lane = lane_iota((rows, LANES))
    total = slots * ncol
    for g, ref in enumerate((prev_ref, own_ref, next_ref)):
        offsets = ref[...].astype(jnp.int32)
        bit = 1
        while bit < ncol:
            step = bit * slots
            swapped = jnp.where((lane // step) % 2 == 1, pltpu.roll(offsets, step, 1),
                                pltpu.roll(offsets, LANES - step, 1))
            offsets = jnp.where((column // bit) % 2 == 1, swapped, offsets)
            bit *= 2
        place = offsets + (row_iota((rows, LANES)) + (g + 1) * rows)
        for s in range(total):
            where = jnp.broadcast_to(place[:, size + s : size + s + 1], (rows, LANES))
            tmp_ref[pl.ds(g * rows * total + s, rows, stride=total), :] = jnp.where(
                where == lane, 1.0, 0.0)
    for j in range(3 * rows):
        hot_ref[j] = tmp_ref[j * total : (j + 1) * total, :].astype(jnp.bfloat16)


def coarse_kernel(size, ncol, scal, offs, *refs):
    blocks = refs[: 3 * ncol]
    unit_ref, hot_ref, hi_ref, lo_ref, out_ref, p_ref, ph_ref, pl_ref, r_ref, t_ref = refs[3 * ncol :]
    rows = hi_ref.shape[0]
    slots = hi_ref.shape[2] // size
    total = slots * ncol
    pairs = slots // 2
    column = scal[0]
    lane = lane_iota((rows, LANES))
    low_half = lane < size
    for g in range(3):
        degree = sum(blocks[g * ncol + d][pairs * rows :, :] for d in range(ncol))
        inverse = relax_weight / jnp.where(low_half, degree, 1.0)
        inverse = jnp.where(low_half, inverse, pltpu.roll(inverse, size, 1))
        own_term = jnp.where(low_half, (1.0 - relax_weight) * unit_ref[g * rows : (g + 1) * rows, :], 0.0)
        for d in range(ncol):
            for p in range(pairs):
                v = blocks[g * ncol + d][p * rows : (p + 1) * rows, :] * inverse
                if p == 0:
                    v = v + jnp.where(column == d, own_term, 0.0)
                w = pltpu.roll(v, size, 1)
                base = g * rows * total + d * slots + 2 * p
                p_ref[pl.ds(base, rows, stride=total), :] = jnp.where(low_half, v, w)
                p_ref[pl.ds(base + 1, rows, stride=total), :] = jnp.where(low_half, w, v)
    for j in range(3 * rows):
        hi, lo = split(p_ref[j * total : (j + 1) * total, :])
        ph_ref[j] = hi
        pl_ref[j] = lo
    tile_half = lane_iota((total, LANES)) // size
    zero = jnp.zeros((total, LANES), jnp.bfloat16)
    targets = [[rows + i + offs[i, column * slots + k] for k in range(slots)] for i in range(rows)]
    for i in range(rows):
        for p in range(pairs):
            his, los = [], []
            for h in range(2):
                t = targets[i][2 * p + h]
                his.append(jnp.where(tile_half == h, ph_ref[t], zero))
                los.append(jnp.where(tile_half == h, pl_ref[t], zero))
            lanes = slice(p * LANES, (p + 1) * LANES)
            high = jnp.concatenate(his, axis=0)
            both = mxu(jnp.concatenate([high] + los, axis=0), hi_ref[i, :, lanes], NT)
            rest = mxu(high, lo_ref[i, :, lanes], NT)
            r_ref[i, 2 * p * total : 2 * (p + 1) * total, :] = -(
                both[: 2 * total] + both[2 * total :] + rest)
    own_degree = blocks[ncol][pairs * rows :, :]
    for i in range(rows):
        j = rows + i
        diagonal = p_ref[j * total : (j + 1) * total, :size] * own_degree[i : i + 1, :size]
        r = jnp.concatenate([r_ref[i], diagonal], axis=0)
        hi, lo = split(jnp.concatenate([r, r], axis=1))
        rhs = jnp.concatenate([hi, lo], axis=1)
        first = jnp.where(tile_half == 0, ph_ref[j], pl_ref[j])
        second = jnp.where(tile_half == 0, ph_ref[j], zero)
        s = mxu(jnp.concatenate([first, second], axis=1), rhs, NT)
        hi, lo = split(s)
        hot = jnp.concatenate([hot_ref[t] for t in targets[i]] + [hot_ref[j]], axis=0)
        both = mxu(jnp.concatenate([hi, lo], axis=0), hot, NN)
        t_ref[i * total : (i + 1) * total, :] = both[:total] + both[total:]
    hi, lo = split(t_ref[...])
    own_hot = hot_ref[rows : 2 * rows].reshape(rows * total, LANES)
    absolute = mxu(own_hot, hi, TN) + mxu(own_hot, lo, TN)
    amount = (BAND // 2 - row_iota((LANES, LANES))) % LANES
    bit = 1
    while bit < LANES:
        absolute = jnp.where((amount // bit) % 2 == 1, pltpu.roll(absolute, bit, 1), absolute)
        bit *= 2
    out_ref[...] = absolute[rows : 4 * rows]


SMEM = pl.BlockSpec(memory_space=pltpu.SMEM)
VMEM = pl.BlockSpec(memory_space=pltpu.VMEM)


def on_device(weights, block_cols, counts, near_null, prior_ridge):
    rows, slots, size, _ = weights.shape
    total = block_cols.shape[1]
    nrow, ncol = lax.axis_size("row"), lax.axis_size("col")
    all_rows = rows * nrow
    first = lax.axis_index("row") * rows
    column = lax.axis_index("col")
    scal = column.reshape(1).astype(jnp.int32)
    local = jnp.arange(rows, dtype=jnp.int32)
    offsets = (block_cols - (first + local)[:, None] + H) % all_rows - H
    f32, bf16 = jnp.float32, jnp.bfloat16

    def to_row(x, by):
        return lax.ppermute(x, "row", [(r, (r + by) % nrow) for r in range(nrow)])

    def to_col(x, d):
        return lax.ppermute(x, "col", [(c, c ^ d) for c in range(ncol)])

    own = jnp.concatenate(
        [near_null, offsets.astype(f32), jnp.zeros((rows, LANES - size - total), f32)], axis=1)
    prev, nxt = to_row(own, 1), to_row(own, -1)
    w_hi, w_lo = pl.pallas_call(
        pack_kernel,
        out_shape=[jax.ShapeDtypeStruct((rows, size, slots * size), bf16)] * 2,
        in_specs=[SMEM, SMEM, VMEM], out_specs=[VMEM] * 2, name="pack",
    )(scal, counts, weights)
    planes = (slots // 2 + 1) * rows
    block, unit = pl.pallas_call(
        functools.partial(unit_kernel, size),
        out_shape=[jax.ShapeDtypeStruct((planes, LANES), f32),
                   jax.ShapeDtypeStruct((3 * rows, LANES), f32)],
        in_specs=[SMEM] * 3 + [VMEM] * 6, out_specs=[VMEM] * 2,
        scratch_shapes=[pltpu.VMEM((8 * rows, size), f32)], name="unit",
    )(scal, offsets, counts, prev, own, nxt, prior_ridge, w_hi, w_lo)
    hot = pl.pallas_call(
        functools.partial(hot_kernel, size, slots, ncol),
        out_shape=jax.ShapeDtypeStruct((3 * rows, total, LANES), bf16),
        in_specs=[SMEM] + [VMEM] * 3, out_specs=VMEM,
        scratch_shapes=[pltpu.VMEM((3 * rows * total, LANES), f32)], name="hot",
    )(scal, prev, own, nxt)
    halo = jnp.stack([to_row(block, 1), block, to_row(block, -1)])
    gathered = [halo] + [to_col(halo, d) for d in range(1, ncol)]
    blocks = [gathered[d][g] for g in range(3) for d in range(ncol)]
    parts = pl.pallas_call(
        functools.partial(coarse_kernel, size, ncol),
        out_shape=jax.ShapeDtypeStruct((3 * rows, LANES), f32),
        in_specs=[SMEM] * 2 + [VMEM] * (3 * ncol + 4), out_specs=VMEM,
        scratch_shapes=[
            pltpu.VMEM((3 * rows * total, LANES), f32),
            pltpu.VMEM((3 * rows, total, LANES), bf16),
            pltpu.VMEM((3 * rows, total, LANES), bf16),
            pltpu.VMEM((rows, slots * total, size), f32),
            pltpu.VMEM((rows * total, LANES), f32),
        ], name="coarse",
    )(scal, offsets, *blocks, unit, hot, w_hi, w_lo)
    own_rows = parts[rows : 2 * rows] + to_row(parts[2 * rows :], 1) + to_row(parts[:rows], -1)
    share = rows // ncol
    mine = lax.dynamic_slice_in_dim(own_rows, column * share, share, 0)
    for d in range(1, ncol):
        mine = mine + to_col(lax.dynamic_slice_in_dim(own_rows, (column ^ d) * share, share, 0), d)
    return mine


def solution(mesh):
    placed = (P("row", "col", None, None), P("row", None), P("row"), P("row", None), P("row", None))
    return jax.shard_map(
        on_device, mesh=mesh, in_specs=placed, out_specs=P(("row", "col"), None), check_vma=False
    )
```

```python
import functools

import jax
import jax.numpy as jnp
from jax import lax
from jax.experimental import pallas as pl
from jax.experimental.pallas import tpu as pltpu
from jax.sharding import PartitionSpec as P


H = 21
BAND = 128
LANES = 128

epsilon = 1e-06
relax_weight = 2.0 / 3.0

NT = (((1,), (1,)), ((), ()))
NN = (((1,), (0,)), ((), ()))
TN = (((0,), (0,)), ((), ()))


def mxu(a, b, dims):
    return lax.dot_general(a, b, dims, preferred_element_type=jnp.float32)


def split(x):
    hi = x.astype(jnp.bfloat16)
    lo = (x - hi.astype(jnp.float32)).astype(jnp.bfloat16)
    return hi, lo


def lane_iota(shape):
    return lax.broadcasted_iota(jnp.int32, shape, len(shape) - 1)


def row_iota(shape):
    return lax.broadcasted_iota(jnp.int32, shape, 0)


def pack_kernel(place, counts, w_ref, hi_ref, lo_ref):
    rows, slots, size, _ = w_ref.shape
    start = place[1] * slots
    per = LANES // size
    for i in range(rows):
        for p in range(slots // per):
            tile = jnp.concatenate([w_ref[i, per * p + h] for h in range(per)], axis=1)
            slot = lane_iota((size, LANES)) // size + (start + per * p)
            tile = jnp.where(slot < counts[i], tile, 0.0)
            hi, lo = split(tile)
            hi_ref[i, :, p * LANES : (p + 1) * LANES] = hi
            lo_ref[i, :, p * LANES : (p + 1) * LANES] = lo


def wrap(x, count):
    x = jnp.where(x < 0, x + count, x)
    return jnp.where(x >= count, x - count, x)


def tile_targets(place, cols, rows, slots, all_rows):
    first, start = place[0] * rows, place[1] * slots
    return [
        [rows + i - H + wrap(cols[i, start + k] - (first + i) + H, all_rows) for k in range(slots)]
        for i in range(rows)
    ]


def unit_kernel(size, all_rows, place, cols, mine_ref, other_ref, own_ref, ridge_ref, hi_ref, lo_ref,
                block_ref, unit_ref, acc_ref):
    rows = own_ref.shape[0]
    slots = hi_ref.shape[2] // size
    column = place[1]
    even = column % 2 == 0
    prev = jnp.where(even, mine_ref[...], other_ref[...])
    after = jnp.where(even, other_ref[...], mine_ref[...])
    for g, x in enumerate((prev, own_ref[...], after)):
        unit = x / jnp.sqrt(jnp.sum(x * x, axis=1, keepdims=True) + epsilon)
        unit_ref[g * rows : (g + 1) * rows, :] = jnp.concatenate([unit, unit], axis=1)
    row8 = row_iota((8, LANES))
    half = lane_iota((8, LANES)) // size
    targets = tile_targets(place, cols, rows, slots, all_rows)
    for i in range(rows):
        parts = []
        for p in range(slots // 2):
            tile = jnp.where(row8 == slots, 1.0, 0.0)
            for h in range(2):
                k = 2 * p + h
                vec = jnp.broadcast_to(unit_ref[pl.ds(targets[i][k], 1), :], (8, LANES))
                tile = jnp.where((row8 == k) & (half == h), vec, tile)
            parts.append(tile)
        lhs = jnp.concatenate(parts, axis=1)
        hi, lo = split(lhs)
        both = mxu(jnp.concatenate([hi, lo], axis=0), hi_ref[i], NT)
        low = mxu(hi, lo_ref[i], NT)
        acc_ref[8 * i : 8 * i + 8, :] = both[:8] + both[8:] + low
    plane = [acc_ref[pl.ds(k, rows, stride=8), :] for k in range(slots + 1)]
    for p in range(slots // 2):
        block_ref[p * rows : (p + 1) * rows, :] = jnp.concatenate(plane[2 * p : 2 * p + 2], axis=1)
    degree = plane[slots] + jnp.where(column == 0, ridge_ref[...], 0.0)
    block_ref[(slots // 2) * rows :, :] = jnp.concatenate([degree, jnp.zeros_like(degree)], axis=1)


def hot_kernel(slots, all_rows, place, mine_ref, other_ref, own_ref, hot_ref, tmp_ref):
    rows, total = own_ref.shape
    column = place[1]
    even = column % 2 == 0
    prev = jnp.where(even, mine_ref[...], other_ref[...])
    after = jnp.where(even, other_ref[...], mine_ref[...])
    lane = lane_iota((rows, LANES))
    for g, cols in enumerate((prev, own_ref[...], after)):
        local = row_iota((rows, LANES)) + (g - 1) * rows
        cols = jnp.concatenate([cols, jnp.zeros((rows, LANES - total), jnp.int32)], axis=1)
        where = wrap(wrap(cols - place[0] * rows - local + H, all_rows), all_rows) - H + local + 2 * rows
        bit = slots
        while bit < total:
            swapped = jnp.where((lane // bit) % 2 == 1, pltpu.roll(where, bit, 1),
                                pltpu.roll(where, LANES - bit, 1))
            where = jnp.where((column * slots // bit) % 2 == 1, swapped, where)
            bit *= 2
        for s in range(total):
            spread = jnp.broadcast_to(where[:, s : s + 1], (rows, LANES))
            tmp_ref[pl.ds(g * rows * total + s, rows, stride=total), :] = jnp.where(
                spread == lane, 1.0, 0.0)
    for j in range(3 * rows):
        hot_ref[j] = tmp_ref[j * total : (j + 1) * total, :].astype(jnp.bfloat16)


def coarse_kernel(size, ncol, nrow, place, cols, own_ref, straight_ref, diagonal_ref, far_ref, last_ref,
                  unit_ref, hot_ref, hi_ref, lo_ref, out_ref, p_ref, ph_ref, pl_ref, r_ref, t_ref):
    rows = hi_ref.shape[0]
    slots = hi_ref.shape[2] // size
    total = slots * ncol
    pairs = slots // 2
    column = place[1]
    low_half = lane_iota((rows, LANES)) < size
    even = column % 2 == 0
    planes = (pairs + 1) * rows
    blocks = [
        [(straight_ref, 0), (straight_ref, 1), (diagonal_ref, 0), (diagonal_ref, 1)],
        [(own_ref, 0), (own_ref, 1), (far_ref, 0), (last_ref, 4)],
        [(last_ref, 1), (last_ref, 0), (last_ref, 3), (last_ref, 2)],
    ]

    def plane(part, d, p):
        ref, index = blocks[part][d]
        return ref[index * planes + p * rows : index * planes + (p + 1) * rows, :]

    groups = (jnp.where(even, 0, 2), 1, jnp.where(even, 2, 0))
    for part, group in enumerate(groups):
        degree = sum(plane(part, d, pairs) for d in range(ncol))
        inverse = relax_weight / jnp.where(low_half, degree, 1.0)
        inverse = jnp.where(low_half, inverse, pltpu.roll(inverse, size, 1))
        unit = unit_ref[pl.ds(pl.multiple_of(group * rows, 8), rows), :]
        own_term = jnp.where(low_half, (1.0 - relax_weight) * unit, 0.0)
        for d in range(ncol):
            for p in range(pairs):
                v = plane(part, d, p) * inverse
                if p == 0:
                    v = v + jnp.where(column == d, own_term, 0.0)
                w = pltpu.roll(v, size, 1)
                base = group * (rows * total) + (d * slots + 2 * p)
                p_ref[pl.ds(base, rows, stride=total), :] = jnp.where(low_half, v, w)
                p_ref[pl.ds(base + 1, rows, stride=total), :] = jnp.where(low_half, w, v)
    for j in range(3 * rows):
        hi, lo = split(p_ref[j * total : (j + 1) * total, :])
        ph_ref[j] = hi
        pl_ref[j] = lo
    tile_half = lane_iota((total, LANES)) // size
    zero = jnp.zeros((total, LANES), jnp.bfloat16)
    targets = tile_targets(place, cols, rows, slots, rows * nrow)
    for i in range(rows):
        for p in range(pairs):
            his, los = [], []
            for h in range(2):
                t = targets[i][2 * p + h]
                his.append(jnp.where(tile_half == h, ph_ref[t], zero))
                los.append(jnp.where(tile_half == h, pl_ref[t], zero))
            lanes = slice(p * LANES, (p + 1) * LANES)
            high = jnp.concatenate(his, axis=0)
            both = mxu(jnp.concatenate([high] + los, axis=0), hi_ref[i, :, lanes], NT)
            rest = mxu(high, lo_ref[i, :, lanes], NT)
            r_ref[i, 2 * p * total : 2 * (p + 1) * total, :] = -(
                both[: 2 * total] + both[2 * total :] + rest)
    own_degree = plane(1, 0, pairs)
    for i in range(rows):
        j = rows + i
        diagonal = p_ref[j * total : (j + 1) * total, :size] * own_degree[i : i + 1, :size]
        r = jnp.concatenate([r_ref[i], diagonal], axis=0)
        hi, lo = split(jnp.concatenate([r, r], axis=1))
        rhs = jnp.concatenate([hi, lo], axis=1)
        first = jnp.where(tile_half == 0, ph_ref[j], pl_ref[j])
        second = jnp.where(tile_half == 0, ph_ref[j], zero)
        s = mxu(jnp.concatenate([first, second], axis=1), rhs, NT)
        hi, lo = split(s)
        hot = jnp.concatenate([hot_ref[t] for t in targets[i]] + [hot_ref[j]], axis=0)
        both = mxu(jnp.concatenate([hi, lo], axis=0), hot, NN)
        t_ref[i * total : (i + 1) * total, :] = both[:total] + both[total:]
    hi, lo = split(t_ref[...])
    own_hot = hot_ref[rows : 2 * rows].reshape(rows * total, LANES)
    absolute = mxu(own_hot, hi, TN) + mxu(own_hot, lo, TN)
    amount = (BAND // 2 - row_iota((LANES, LANES))) % LANES
    bit = 1
    while bit < LANES:
        absolute = jnp.where((amount // bit) % 2 == 1, pltpu.roll(absolute, bit, 1), absolute)
        bit *= 2
    share = rows // ncol
    out_ref[...] = jnp.zeros_like(out_ref)
    for g in range(3):
        row = wrap(place[0] + (g - 1), nrow)
        for c in range(ncol):
            at = (g + 1) * rows + c * share
            out_ref[row * ncol + c] = absolute[at : at + share]


def sum_kernel(ncol, nrow, place, got_ref, out_ref):
    total = None
    for g in range(3):
        row = wrap(place[0] + (g - 1), nrow)
        for c in range(ncol):
            part = got_ref[row * ncol + c]
            total = part if total is None else total + part
    out_ref[...] = total


SMEM = pl.BlockSpec(memory_space=pltpu.SMEM)
VMEM = pl.BlockSpec(memory_space=pltpu.VMEM)
VMEM_LIMIT = 20 * 1024 * 1024


def on_device(weights, block_cols, counts, near_null, prior_ridge):
    rows, slots, size, _ = weights.shape
    total = block_cols.shape[1]
    nrow, ncol = lax.axis_size("row"), lax.axis_size("col")
    all_rows = rows * nrow
    f32, bf16 = jnp.float32, jnp.bfloat16
    place = jnp.stack([lax.axis_index("row"), lax.axis_index("col")]).astype(jnp.int32)

    def call(kernel, out_shape, smem, vmem, scratch, *operands):
        return pl.pallas_call(
            kernel, out_shape=out_shape, in_specs=[SMEM] * smem + [VMEM] * vmem,
            out_specs=jax.tree.map(lambda _: VMEM, out_shape), scratch_shapes=scratch,
            compiler_params=pltpu.CompilerParams(vmem_limit_bytes=VMEM_LIMIT),
        )(*operands)

    def send(x, to):
        pairs = []
        for r in range(nrow):
            for c in range(ncol):
                nr, nc = to(r, c)
                pairs.append((r * ncol + c, (nr % nrow) * ncol + nc))
        return lax.ppermute(x, ("row", "col"), pairs)

    def partner(x):
        return send(x, lambda r, c: (r, c ^ 1))

    def across(x):
        return send(x, lambda r, c: (r, c ^ 2))

    def outward(x, d=0):
        return send(x, lambda r, c: (r + (1 if c % 2 == 0 else -1), c ^ d))

    null_mine = outward(near_null)
    cols_mine = outward(block_cols)
    w_hi, w_lo = call(
        pack_kernel, [jax.ShapeDtypeStruct((rows, size, slots * size), bf16)] * 2, 2, 1, [],
        place, counts, weights)
    null_other = partner(null_mine)
    cols_other = partner(cols_mine)
    planes = (slots // 2 + 1) * rows
    block, unit = call(
        functools.partial(unit_kernel, size, all_rows),
        [jax.ShapeDtypeStruct((planes, LANES), f32), jax.ShapeDtypeStruct((3 * rows, LANES), f32)],
        2, 6, [pltpu.VMEM((8 * rows, size), f32)],
        place, block_cols, null_mine, null_other, near_null, prior_ridge, w_hi, w_lo)
    hot = call(
        functools.partial(hot_kernel, slots, all_rows),
        jax.ShapeDtypeStruct((3 * rows, total, LANES), bf16), 1, 3,
        [pltpu.VMEM((3 * rows * total, LANES), f32)],
        place, cols_mine, cols_other, block_cols)
    pair = partner(block)
    far = across(block)
    own = jnp.concatenate([block, pair])
    diagonal = outward(own, 2)
    straight = outward(own)
    last = partner(jnp.concatenate([straight, diagonal, far]))
    parts = call(
        functools.partial(coarse_kernel, size, ncol, nrow),
        jax.ShapeDtypeStruct((nrow * ncol, rows // ncol, LANES), f32), 2, 9,
        [
            pltpu.VMEM((3 * rows * total, LANES), f32),
            pltpu.VMEM((3 * rows, total, LANES), bf16),
            pltpu.VMEM((3 * rows, total, LANES), bf16),
            pltpu.VMEM((rows, slots * total, size), f32),
            pltpu.VMEM((rows * total, LANES), f32),
        ],
        place, block_cols, own, straight, diagonal, far, last, unit, hot, w_hi, w_lo)
    got = lax.all_to_all(parts, ("row", "col"), 0, 0)
    return call(
        functools.partial(sum_kernel, ncol, nrow), jax.ShapeDtypeStruct((rows // ncol, LANES), f32),
        1, 1, [], place, got)


def solution(mesh):
    placed = (P("row", "col", None, None), P("row", None), P("row"), P("row", None), P("row", None))

    return jax.shard_map(
        on_device, mesh=mesh, in_specs=placed, out_specs=P(("row", "col"), None), check_vma=False
    )
```

```python
import functools

import jax
import jax.numpy as jnp
from jax import lax
from jax.experimental import pallas as pl
from jax.experimental.pallas import tpu as pltpu
from jax.sharding import PartitionSpec as P


H = 21
BAND = 128
LANES = 128

epsilon = 1e-06
relax_weight = 2.0 / 3.0

NT = (((1,), (1,)), ((), ()))
NN = (((1,), (0,)), ((), ()))


def mxu(a, b, dims):
    return lax.dot_general(a, b, dims, preferred_element_type=jnp.float32)


def split(x):
    hi = x.astype(jnp.bfloat16)
    lo = (x - hi.astype(jnp.float32)).astype(jnp.bfloat16)
    return hi, lo


def lane_iota(shape):
    return lax.broadcasted_iota(jnp.int32, shape, len(shape) - 1)


def row_iota(shape):
    return lax.broadcasted_iota(jnp.int32, shape, 0)


def wrap(x, count):
    x = jnp.where(x < 0, x + count, x)
    return jnp.where(x >= count, x - count, x)


def roll(x, by):
    return pltpu.roll(x, by % LANES, 1)


def pack_kernel(all_rows, counts_hbm, w_hbm, cols_hbm, hi_ref, lo_ref, target_ref, counts, cols_ref,
                w_ref, sems):
    rows, slots, size, _ = w_ref.shape
    start = lax.axis_index("col") * slots
    per = LANES // size
    chunks = sems.shape[0] - 2
    step = rows // chunks
    small = [
        pltpu.make_async_copy(counts_hbm, counts, sems.at[chunks]),
        pltpu.make_async_copy(cols_hbm, cols_ref, sems.at[chunks + 1]),
    ]
    copies = [
        pltpu.make_async_copy(w_hbm.at[pl.ds(n * step, step)], w_ref.at[pl.ds(n * step, step)], sems.at[n])
        for n in range(chunks)
    ]
    for copy in small + copies:
        copy.start()
    for copy in small:
        copy.wait()
    cols = cols_ref[...]
    local = lane_iota(cols.shape)
    first = lax.axis_index("row") * rows
    target_ref[...] = wrap(cols - (first + local) + H, all_rows) + (rows - H) + local
    for i in range(rows):
        if i % step == 0:
            copies[i // step].wait()
        for p in range(slots // per):
            tile = jnp.concatenate([w_ref[i, per * p + h] for h in range(per)], axis=1)
            slot = lane_iota((size, LANES)) // size + (start + per * p)
            tile = jnp.where(slot < counts[i], tile, 0.0)
            hi, lo = split(tile)
            hi_ref[i, :, p * LANES : (p + 1) * LANES] = hi
            lo_ref[i, :, p * LANES : (p + 1) * LANES] = lo


def unit_kernel(size, targets, mine_ref, other_ref, own_ref, ridge_ref, hi_ref, lo_ref,
                block_ref, unit_ref, acc_ref):
    rows = own_ref.shape[0]
    slots = hi_ref.shape[2] // size
    column = lax.axis_index("col")
    even = column % 2 == 0
    prev = jnp.where(even, mine_ref[...], other_ref[...])
    after = jnp.where(even, other_ref[...], mine_ref[...])
    for g, x in enumerate((prev, own_ref[...], after)):
        unit = x / jnp.sqrt(jnp.sum(x * x, axis=1, keepdims=True) + epsilon)
        unit_ref[g * rows : (g + 1) * rows, :] = jnp.concatenate([unit, unit], axis=1)
    row8 = row_iota((8, LANES))
    half = lane_iota((8, LANES)) // size
    for i in range(rows):
        parts = []
        for p in range(slots // 2):
            tile = jnp.where(row8 == slots, 1.0, 0.0)
            for h in range(2):
                k = 2 * p + h
                vec = jnp.broadcast_to(unit_ref[pl.ds(targets[column * slots + k, i], 1), :], (8, LANES))
                tile = jnp.where((row8 == k) & (half == h), vec, tile)
            parts.append(tile)
        lhs = jnp.concatenate(parts, axis=1)
        hi, lo = split(lhs)
        both = mxu(jnp.concatenate([hi, lo], axis=0), hi_ref[i], NT)
        low = mxu(hi, lo_ref[i], NT)
        acc_ref[8 * i : 8 * i + 8, :] = both[:8] + both[8:] + low
    plane = [acc_ref[pl.ds(k, rows, stride=8), :] for k in range(slots + 1)]
    for p in range(slots // 2):
        block_ref[p * rows : (p + 1) * rows, :] = jnp.concatenate(plane[2 * p : 2 * p + 2], axis=1)
    degree = plane[slots] + jnp.where(column == 0, ridge_ref[...], 0.0)
    block_ref[(slots // 2) * rows :, :] = jnp.concatenate([degree, jnp.zeros_like(degree)], axis=1)


def hot_kernel(slots, all_rows, mine_ref, other_ref, own_ref, even_ref, odd_ref, turned_ref,
               even_tmp, odd_tmp):
    total, rows = own_ref.shape
    column = lax.axis_index("col")
    even = column % 2 == 0
    prev = jnp.where(even, mine_ref[...], other_ref[...])
    after = jnp.where(even, other_ref[...], mine_ref[...])
    lane = lane_iota((rows, LANES))
    pairs = total // 2
    for g, cols in enumerate((prev, own_ref[...], after)):
        local = row_iota((rows, LANES)) + (g - 1) * rows
        cols = jnp.concatenate([cols, jnp.zeros((total, LANES - rows), jnp.int32)], axis=1)
        cols = jnp.concatenate([cols, jnp.zeros((LANES - total, LANES), jnp.int32)], axis=0)
        cols = cols.T[:rows]
        base = lax.axis_index("row") * rows + local
        where = wrap(wrap(cols - base + H, all_rows), all_rows) - H + local + 2 * rows
        bit = slots
        while bit < total:
            swapped = jnp.where((lane // bit) % 2 == 1, roll(where, bit), roll(where, -bit))
            where = jnp.where((column * slots // bit) % 2 == 1, swapped, where)
            bit *= 2
        for s in range(total):
            spread = jnp.broadcast_to(where[:, s : s + 1], (rows, LANES))
            hot = jnp.where(spread == lane, 1.0, 0.0)
            at, other = s // 2 + (s % 2) * pairs, s // 2 + (1 - s % 2) * pairs
            even_tmp[pl.ds(g * rows * total + at, rows, stride=total), :] = hot
            odd_tmp[pl.ds(g * rows * total + other, rows, stride=total), :] = hot
    for j in range(3 * rows):
        even_ref[j] = even_tmp[j * total : (j + 1) * total, :].astype(jnp.bfloat16)
        odd_ref[j] = odd_tmp[j * total : (j + 1) * total, :].astype(jnp.bfloat16)
    for n in range(rows * total // LANES):
        at = rows * total + n * LANES
        turned = even_tmp[at : at + LANES, :].T
        turned_ref[:, n * LANES : (n + 1) * LANES] = turned[rows : 4 * rows].astype(jnp.bfloat16)


def coarse_kernel(size, ncol, nrow, targets, own_ref, straight_ref, diagonal_ref, far_ref, last_ref,
                  unit_ref, even_ref, odd_ref, turned_ref, hi_ref, lo_ref, out_ref,
                  p_ref, q_ref, qh_ref, ql_ref, rh_ref, rl_ref, s_ref, th_ref, tl_ref):
    rows = hi_ref.shape[0]
    slots = hi_ref.shape[2] // size
    total = slots * ncol
    pairs = slots // 2
    half = total // 2
    column = lax.axis_index("col")
    low_half = lane_iota((rows, LANES)) < size
    even = column % 2 == 0
    planes = (pairs + 1) * rows
    blocks = [
        [(straight_ref, 0), (straight_ref, 1), (diagonal_ref, 0), (diagonal_ref, 1)],
        [(own_ref, 0), (own_ref, 1), (far_ref, 0), (last_ref, 4)],
        [(last_ref, 1), (last_ref, 0), (last_ref, 3), (last_ref, 2)],
    ]

    def plane(part, d, p):
        ref, index = blocks[part][d]
        return ref[index * planes + p * rows : index * planes + (p + 1) * rows, :]

    for part, group in enumerate((jnp.where(even, 0, 2), 1, jnp.where(even, 2, 0))):
        degree = sum(plane(part, d, pairs) for d in range(ncol))
        inverse = relax_weight / jnp.where(low_half, degree, 1.0)
        inverse = jnp.where(low_half, inverse, roll(inverse, size))
        unit = unit_ref[pl.ds(pl.multiple_of(group * rows, 8), rows), :]
        own_term = jnp.where(low_half, (1.0 - relax_weight) * unit, 0.0)
        for d in range(ncol):
            for p in range(pairs):
                v = plane(part, d, p) * inverse
                if p == 0:
                    v = v + jnp.where(column == d, own_term, 0.0)
                p_ref[pl.ds(group * (rows * half) + (d * pairs + p), rows, stride=half), :] = v
    for j in range(3 * rows):
        v = p_ref[j * half : (j + 1) * half, :]
        q = jnp.concatenate([v, roll(v, size)], axis=0)
        if rows <= j < 2 * rows:
            q_ref[j - rows] = q
        qh_ref[j], ql_ref[j] = split(q)
    tile_half = lane_iota((total, LANES)) // size
    zero = jnp.zeros((total, LANES), jnp.bfloat16)
    tiles = [[targets[column * slots + k, i] for k in range(slots)] for i in range(rows)]
    for i in range(rows):
        for p in range(pairs):
            his, los = [], []
            for h in range(2):
                t = tiles[i][2 * p + h]
                his.append(jnp.where(tile_half == h, qh_ref[t], zero))
                los.append(jnp.where(tile_half == h, ql_ref[t], zero))
            lanes = slice(p * LANES, (p + 1) * LANES)
            high = jnp.concatenate(his, axis=0)
            both = mxu(jnp.concatenate([high] + los, axis=0), hi_ref[i, :, lanes], NT)
            rest = mxu(high, lo_ref[i, :, lanes], NT)
            at = slice(2 * p * total, 2 * (p + 1) * total)
            rh_ref[i, at, :], rl_ref[i, at, :] = split(both[: 2 * total] + both[2 * total :] + rest)
    own_degree = plane(1, 0, pairs)
    for i in range(rows):
        diagonal = q_ref[i, :, :size] * own_degree[i : i + 1, :size]
        rh_ref[i, slots * total :, :], rl_ref[i, slots * total :, :] = split(diagonal)
    sign = jnp.where(lane_iota((total, (slots + 1) * total)) < slots * total, -1.0, 1.0)
    for i in range(rows):
        j = rows + i
        left = qh_ref[j, :, :size]
        both = mxu(jnp.concatenate([left, ql_ref[j, :, :size]], axis=0), rh_ref[i], NT)
        s = (both[:total] + both[total:] + mxu(left, rl_ref[i], NT)) * sign
        s_ref[i, :total, :], s_ref[i, total:, :] = split(s)
    for i in range(rows):
        hot = [(even_ref if k % 2 == 0 else odd_ref)[tiles[i][k]] for k in range(slots)]
        both = mxu(s_ref[i], jnp.concatenate(hot + [even_ref[rows + i]], axis=0), NN)
        at = slice(i * total, (i + 1) * total)
        th_ref[at, :], tl_ref[at, :] = split(both[:total] + both[total:])
    turned = turned_ref[...]
    absolute = mxu(turned, th_ref[...], NN) + mxu(turned, tl_ref[...], NN)
    share = rows // ncol
    out_ref[...] = jnp.zeros_like(out_ref)
    for g in range(3):
        row = wrap(lax.axis_index("row") + (g - 1), nrow)
        part = roll(absolute[g * rows : (g + 1) * rows], (1 - g) * rows)
        for c in range(ncol):
            out_ref[row * ncol + c] = part[c * share : (c + 1) * share]


def sum_kernel(ncol, nrow, got_ref, out_ref):
    share = out_ref.shape[0]
    total = None
    for g in range(3):
        row = wrap(lax.axis_index("row") + (g - 1), nrow)
        for c in range(ncol):
            part = got_ref[row * ncol + c]
            total = part if total is None else total + part
    local = row_iota(total.shape) + lax.axis_index("col") * share
    amount = (BAND // 2 - 2 * share * ncol - local) % LANES
    bit = 1
    while bit < LANES:
        total = jnp.where((amount // bit) % 2 == 1, roll(total, bit), total)
        bit *= 2
    out_ref[...] = total


HBM = pl.BlockSpec(memory_space=pltpu.HBM)
SMEM = pl.BlockSpec(memory_space=pltpu.SMEM)
VMEM = pl.BlockSpec(memory_space=pltpu.VMEM)
VMEM_LIMIT = 20 * 1024 * 1024
PACK_LIMIT = 51 * 1024 * 1024
CHUNKS = 6


def on_device(weights, block_cols, counts, near_null, prior_ridge):
    rows, slots, size, _ = weights.shape
    total = block_cols.shape[1]
    nrow, ncol = lax.axis_size("row"), lax.axis_size("col")
    all_rows = rows * nrow
    f32, bf16, i32 = jnp.float32, jnp.bfloat16, jnp.int32
    array = jax.ShapeDtypeStruct
    scratch = pltpu.VMEM

    def call(kernel, out_shape, specs, scratches, *operands, limit=VMEM_LIMIT):
        return pl.pallas_call(
            kernel, out_shape=out_shape, in_specs=specs,
            out_specs=jax.tree.map(lambda _: VMEM, out_shape), scratch_shapes=scratches,
            compiler_params=pltpu.CompilerParams(vmem_limit_bytes=limit),
        )(*operands)

    def send(x, to):
        pairs = []
        for r in range(nrow):
            for c in range(ncol):
                nr, nc = to(r, c)
                pairs.append((r * ncol + c, (nr % nrow) * ncol + nc))
        return lax.ppermute(x, ("row", "col"), pairs)

    def partner(x):
        return send(x, lambda r, c: (r, c ^ 1))

    def across(x):
        return send(x, lambda r, c: (r, c ^ 2))

    def outward(x, d=0):
        return send(x, lambda r, c: (r + (1 if c % 2 == 0 else -1), c ^ d))

    cols = block_cols.T
    null_mine = outward(near_null)
    cols_mine = outward(cols)
    w_hi, w_lo, targets = call(
        functools.partial(pack_kernel, all_rows),
        [array((rows, size, slots * size), bf16)] * 2 + [array((total, rows), i32)],
        [HBM] * 3,
        [
            pltpu.SMEM((rows,), i32), scratch((total, rows), i32), scratch(weights.shape, f32),
            pltpu.SemaphoreType.DMA((2 + (CHUNKS if rows % CHUNKS == 0 else 1),)),
        ],
        counts, weights, cols, limit=PACK_LIMIT)
    null_other = partner(null_mine)
    cols_other = partner(cols_mine)
    planes = (slots // 2 + 1) * rows
    block, unit = call(
        functools.partial(unit_kernel, size),
        [array((planes, LANES), f32), array((3 * rows, LANES), f32)],
        [SMEM] + [VMEM] * 6, [scratch((8 * rows, size), f32)],
        targets, null_mine, null_other, near_null, prior_ridge, w_hi, w_lo)
    hots = call(
        functools.partial(hot_kernel, slots, all_rows),
        [array((3 * rows, total, LANES), bf16)] * 2 + [array((3 * rows, rows * total), bf16)],
        [VMEM] * 3, [scratch((3 * rows * total, LANES), f32)] * 2,
        cols_mine, cols_other, cols)
    own = jnp.concatenate([block, partner(block)])
    diagonal = outward(own, 2)
    straight = outward(own)
    far = across(block)
    last = partner(jnp.concatenate([straight, diagonal, far]))
    parts = call(
        functools.partial(coarse_kernel, size, ncol, nrow),
        array((nrow * ncol, rows // ncol, LANES), f32), [SMEM] + [VMEM] * 11,
        [
            scratch((3 * rows * total // 2, LANES), f32),
            scratch((rows, total, LANES), f32),
            scratch((3 * rows, total, LANES), bf16),
            scratch((3 * rows, total, LANES), bf16),
            scratch((rows, (slots + 1) * total, size), bf16),
            scratch((rows, (slots + 1) * total, size), bf16),
            scratch((rows, 2 * total, (slots + 1) * total), bf16),
            scratch((rows * total, LANES), bf16),
            scratch((rows * total, LANES), bf16),
        ],
        targets, own, straight, diagonal, far, last, unit, *hots, w_hi, w_lo)
    got = lax.all_to_all(parts, ("row", "col"), 0, 0)
    return call(
        functools.partial(sum_kernel, ncol, nrow), array((rows // ncol, LANES), f32), [VMEM], [], got)


def solution(mesh):
    placed = (P("row", "col", None, None), P("row", None), P("row"), P("row", None), P("row", None))

    return jax.shard_map(
        on_device, mesh=mesh, in_specs=placed, out_specs=P(("row", "col"), None), check_vma=False
    )
```

```python
import functools

import jax
import jax.numpy as jnp
from jax import lax
from jax.experimental import pallas as pl
from jax.experimental.pallas import tpu as pltpu
from jax.sharding import PartitionSpec as P


H = 21
BAND = 128
LANES = 128

epsilon = 1e-06
relax_weight = 2.0 / 3.0

NT = (((1,), (1,)), ((), ()))
NN = (((1,), (0,)), ((), ()))


def mxu(a, b, dims):
    return lax.dot_general(a, b, dims, preferred_element_type=jnp.float32)


def split(x):
    hi = x.astype(jnp.bfloat16)
    lo = (x - hi.astype(jnp.float32)).astype(jnp.bfloat16)
    return hi, lo


def lane_iota(shape):
    return lax.broadcasted_iota(jnp.int32, shape, len(shape) - 1)


def row_iota(shape):
    return lax.broadcasted_iota(jnp.int32, shape, 0)


def wrap(x, count):
    x = jnp.where(x < 0, x + count, x)
    return jnp.where(x >= count, x - count, x)


def roll(x, by):
    return pltpu.roll(x, by % LANES, 1)


def pack_kernel(w_hbm, pack_ref, w_ref, sems):
    rows, slots, size, _ = w_ref.shape
    per = LANES // size
    chunks = sems.shape[0]
    step = rows // chunks
    copies = [
        pltpu.make_async_copy(w_hbm.at[pl.ds(n * step, step)], w_ref.at[pl.ds(n * step, step)], sems.at[n])
        for n in range(chunks)
    ]
    for copy in copies:
        copy.start()
    for i in range(rows):
        if i % step == 0:
            copies[i // step].wait()
        for p in range(slots // per):
            tile = jnp.concatenate([w_ref[i, per * p + h] for h in range(per)], axis=1)
            hi, lo = split(tile)
            pack_ref[i, :, 2 * p * LANES : (2 * p + 1) * LANES] = hi
            pack_ref[i, :, (2 * p + 1) * LANES : 2 * (p + 1) * LANES] = lo


def two_part(hi, lo):
    top = jnp.concatenate([hi, hi], axis=1)
    return jnp.concatenate([top, jnp.concatenate([lo, jnp.zeros_like(lo)], axis=1)], axis=0)


def aim_kernel(all_rows, counts_ref, cols_ref, target_ref):
    total, rows = cols_ref.shape
    local = lane_iota((total, rows))
    first = lax.axis_index("row") * rows
    at = wrap(cols_ref[...] - (first + local) + H, all_rows) + (rows - H) + local
    mirror = jnp.where(at < rows, at + 2 * rows, jnp.where(at >= 2 * rows, at - 2 * rows, at))
    at = jnp.where(lax.axis_index("col") % 2 == 0, at, mirror)
    target_ref[...] = jnp.where(row_iota((total, rows)) < counts_ref[...], at, 3 * rows)


def unit_kernel(size, targets, mine_ref, other_ref, own_ref, ridge_ref, pack_ref,
                block_ref, unit_ref, acc_ref):
    rows = own_ref.shape[0]
    slots = pack_ref.shape[2] // (2 * size)
    column = lax.axis_index("col")
    for g, ref in enumerate((mine_ref, own_ref, other_ref)):
        x = ref[...]
        unit = x / jnp.sqrt(jnp.sum(x * x, axis=1, keepdims=True) + epsilon)
        unit_ref[g * rows : (g + 1) * rows, :] = jnp.concatenate([unit, unit], axis=1)
    unit_ref[3 * rows :, :] = jnp.zeros((8, LANES), jnp.float32)
    row8 = row_iota((8, LANES))
    half = lane_iota((8, LANES)) // size
    for i in range(rows):
        both = None
        for p in range(slots // 2):
            tile = jnp.zeros((8, LANES), jnp.float32)
            for h in range(2):
                k = 2 * p + h
                t = targets[column * slots + k, i]
                vec = jnp.broadcast_to(unit_ref[pl.ds(t, 1), :], (8, LANES))
                one = jnp.where(t < 3 * rows, 1.0, 0.0)
                tile = jnp.where((row8 == k) & (half == h), vec, tile)
                tile = jnp.where((row8 == slots) & (half == h), one, tile)
            term = mxu(two_part(*split(tile)), pack_ref[i, :, 2 * p * LANES : 2 * (p + 1) * LANES], NT)
            both = term if both is None else both + term
        acc_ref[8 * i : 8 * i + 8, :] = both[:8] + both[8:]
    plane = [acc_ref[pl.ds(k, rows, stride=8), :] for k in range(slots + 1)]
    for p in range(slots // 2):
        block_ref[p * rows : (p + 1) * rows, :] = jnp.concatenate(plane[2 * p : 2 * p + 2], axis=1)
    degree = plane[slots] + jnp.where(column == 0, ridge_ref[...], 0.0)
    keep = block_ref.shape[0] - (slots // 2) * rows
    rest = jnp.concatenate([degree[keep:], jnp.zeros((2 * keep - rows, size), jnp.float32)], axis=0)
    block_ref[(slots // 2) * rows :, :] = jnp.concatenate([degree[:keep], rest], axis=1)


def hot_kernel(slots, all_rows, mine_ref, other_ref, own_ref, even_ref, odd_ref, turned_ref,
               even_tmp, odd_tmp, turn_tmp):
    total, rows = own_ref.shape
    column = lax.axis_index("col")
    reach = jnp.where(column % 2 == 0, rows, -rows)
    lane = lane_iota((rows, LANES))
    pairs = total // 2
    for g, ref in enumerate((mine_ref, own_ref, other_ref)):
        cols = ref[...]
        local = row_iota((rows, LANES)) + (g - 1) * reach
        cols = jnp.concatenate([cols, jnp.zeros((total, LANES - rows), jnp.int32)], axis=1)
        cols = jnp.concatenate([cols, jnp.zeros((LANES - total, LANES), jnp.int32)], axis=0)
        cols = cols.T[:rows]
        base = lax.axis_index("row") * rows + local
        where = wrap(wrap(cols - base + H, all_rows), all_rows) - H + local + 2 * rows
        bit = slots
        while bit < total:
            swapped = jnp.where((lane // bit) % 2 == 1, roll(where, bit), roll(where, -bit))
            where = jnp.where((column * slots // bit) % 2 == 1, swapped, where)
            bit *= 2
        for s in range(total):
            spread = jnp.broadcast_to(where[:, s : s + 1], (rows, LANES))
            hot = jnp.where(spread == lane, 1.0, 0.0)
            at, other = s // 2 + (s % 2) * pairs, s // 2 + (1 - s % 2) * pairs
            even_tmp[pl.ds(g * rows * total + at, rows, stride=total), :] = hot
            odd_tmp[pl.ds(g * rows * total + other, rows, stride=total), :] = hot
            if g == 1:
                turn_tmp[pl.ds(at, rows, stride=total), :] = jnp.where(
                    spread == LANES - 1 - lane, 1.0, 0.0)
    for j in range(3 * rows):
        even_ref[j] = even_tmp[j * total : (j + 1) * total, :].astype(jnp.bfloat16)
        odd_ref[j] = odd_tmp[j * total : (j + 1) * total, :].astype(jnp.bfloat16)
    even_ref[3 * rows] = jnp.zeros((total, LANES), jnp.bfloat16)
    odd_ref[3 * rows] = jnp.zeros((total, LANES), jnp.bfloat16)
    for n in range(rows * total // LANES):
        lanes = slice(n * LANES, (n + 1) * LANES)
        turned = turn_tmp[lanes, :].T
        turned_ref[:, lanes] = turned[LANES - 4 * rows : LANES - rows].astype(jnp.bfloat16)


def prolong_rows(planes, unit, column, slots, size, p_ref, first, store):
    rows, ncol = unit.shape[0], len(planes)
    pairs = slots // 2
    half = pairs * ncol
    low_half = lane_iota((rows, LANES)) < size
    degree = sum(block(pairs * rows, None) for block in planes)
    keep = degree.shape[0]
    degree = jnp.concatenate([degree, roll(degree, size)[: rows - keep]], axis=0)
    inverse = relax_weight / jnp.where(low_half, degree, 1.0)
    inverse = jnp.where(low_half, inverse, roll(inverse, size))
    own_term = jnp.where(low_half, (1.0 - relax_weight) * unit, 0.0)
    for d in range(ncol):
        for p in range(pairs):
            v = planes[d](p * rows, (p + 1) * rows) * inverse
            if p == 0:
                v = v + jnp.where(column == d, own_term, 0.0)
            p_ref[pl.ds(first * half + d * pairs + p, rows, stride=half), :] = v
    for j in range(first, first + rows):
        v = p_ref[j * half : (j + 1) * half, :]
        store(j, jnp.concatenate([v, roll(v, size)], axis=0))


def block_of(ref, index, size):
    def rows_of(start, stop):
        return ref[index * size + start : index * size + (size if stop is None else stop), :]

    return rows_of


def ready_kernel(size, slots, straight_ref, diagonal_ref, own_ref, far_ref, far_partner_ref, unit_ref,
                 qh_ref, ql_ref, left_ref, diagonal_term_ref, p_ref):
    count = far_ref.shape[0]
    rows, total, _ = diagonal_term_ref.shape
    column = lax.axis_index("col")
    degree = own_ref[(slots // 2) * rows : count, :]
    degree = jnp.concatenate([degree, roll(degree, size)[: rows - degree.shape[0]]], axis=0)
    low_half = lane_iota((total, LANES)) < size
    groups = (
        [(straight_ref, 0), (straight_ref, 1), (diagonal_ref, 0), (diagonal_ref, 1)],
        [(own_ref, 0), (own_ref, 1), (far_ref, 0), (far_partner_ref, 0)],
    )

    def store(j, q):
        qh_ref[j], ql_ref[j] = split(q)
        if j >= rows:
            i = j - rows
            hi, lo = split(jnp.where(low_half, q, roll(q, size)))
            left_ref[i, :total, :] = hi
            left_ref[i, total:, :] = jnp.where(low_half, lo, jnp.zeros_like(lo))
            term = q[:, :size] * degree[i : i + 1, :size]
            diagonal_term_ref[i] = jnp.concatenate(split(term), axis=1)

    for g, group in enumerate(groups):
        blocks = [block_of(ref, index, count) for ref, index in group]
        unit = unit_ref[g * rows : (g + 1) * rows, :]
        prolong_rows(blocks, unit, column, slots, size, p_ref, g * rows, store)


def coarse_kernel(size, ncol, nrow, targets, last_ref, unit_ref, ready_h_ref, ready_l_ref, left_ref,
                  diagonal_term_ref, even_ref, odd_ref, turned_ref, pack_ref, out_ref,
                  p_ref, qh_ref, ql_ref, r_ref, s_ref, t_ref):
    rows = pack_ref.shape[0]
    slots = pack_ref.shape[2] // (2 * size)
    total = slots * ncol
    pairs = slots // 2
    column = lax.axis_index("col")
    count = last_ref.shape[0] // ncol

    def store(j, q):
        qh_ref[2 * rows + j], ql_ref[2 * rows + j] = split(q)

    blocks = [block_of(last_ref, d ^ 1, count) for d in range(ncol)]
    prolong_rows(blocks, unit_ref[2 * rows : 3 * rows, :], column, slots, size, p_ref, 0, store)
    for table, ready in ((qh_ref, ready_h_ref), (ql_ref, ready_l_ref)):
        table[: 2 * rows] = ready[...]
        table[3 * rows] = jnp.zeros((total, LANES), jnp.bfloat16)
    tile_half = lane_iota((total, LANES)) // size
    zero = jnp.zeros((total, LANES), jnp.bfloat16)
    tiles = [[targets[column * slots + k, i] for k in range(slots)] for i in range(rows)]
    for i in range(rows):
        for p in range(pairs):
            his, los = [], []
            for h in range(2):
                t = tiles[i][2 * p + h]
                his.append(jnp.where(tile_half == h, qh_ref[t], zero))
                los.append(jnp.where(tile_half == h, ql_ref[t], zero))
            lhs = two_part(jnp.concatenate(his, axis=0), jnp.concatenate(los, axis=0))
            both = mxu(lhs, pack_ref[i, :, 2 * p * LANES : 2 * (p + 1) * LANES], NT)
            hi, lo = split(both[: 2 * total] + both[2 * total :])
            at = slice(2 * p * total, 2 * (p + 1) * total)
            r_ref[i, at, :] = jnp.concatenate([hi, lo], axis=1)
        r_ref[i, slots * total :, :] = diagonal_term_ref[i]
    sign = jnp.where(lane_iota((total, (slots + 1) * total)) < slots * total, -1.0, 1.0)
    for i in range(rows):
        both = mxu(left_ref[i], r_ref[i], NT)
        s_ref[i, :total, :], s_ref[i, total:, :] = split((both[:total] + both[total:]) * sign)
    for i in range(rows):
        hot = [(even_ref if k % 2 == 0 else odd_ref)[tiles[i][k]] for k in range(slots)]
        both = mxu(s_ref[i], jnp.concatenate(hot + [even_ref[rows + i]], axis=0), NN)
        at = slice(i * total, (i + 1) * total)
        t_ref[at, :LANES], t_ref[at, LANES:] = split(both[:total] + both[total:])
    both = mxu(turned_ref[...], t_ref[...], NN)
    absolute = both[:, :LANES] + both[:, LANES:]
    relative = [
        pltpu.roll(absolute[n : n + 8], (BAND // 2 - 4 * rows + 1 + n) % LANES, 1, stride=1, stride_axis=0)
        for n in range(0, 3 * rows, 8)
    ]
    relative = jnp.concatenate(relative, axis=0)
    share = rows // ncol
    out_ref[...] = jnp.zeros_like(out_ref)
    for g in range(3):
        row = wrap(lax.axis_index("row") + (g - 1), nrow)
        for c in range(ncol):
            at = (3 - g) * rows - (c + 1) * share
            out_ref[row * ncol + c] = relative[at : at + share]


def sum_kernel(ncol, nrow, got_ref, out_ref):
    total = None
    for step in (-1, 0, 1):
        row = wrap(lax.axis_index("row") + step, nrow)
        for c in range(ncol):
            part = got_ref[row * ncol + c]
            total = part if total is None else total + part
    for n in range(total.shape[0]):
        out_ref[n : n + 1, :] = total[total.shape[0] - 1 - n : total.shape[0] - n]


HBM = pl.BlockSpec(memory_space=pltpu.HBM)
SMEM = pl.BlockSpec(memory_space=pltpu.SMEM)
VMEM = pl.BlockSpec(memory_space=pltpu.VMEM)
VMEM_LIMIT = 20 * 1024 * 1024
PACK_LIMIT = 51 * 1024 * 1024
CHUNKS = 6


def on_device(weights, block_cols, counts, near_null, prior_ridge):
    rows, slots, size, _ = weights.shape
    total = block_cols.shape[1]
    nrow, ncol = lax.axis_size("row"), lax.axis_size("col")
    all_rows = rows * nrow
    f32, bf16, i32 = jnp.float32, jnp.bfloat16, jnp.int32
    array = jax.ShapeDtypeStruct
    scratch = pltpu.VMEM

    def call(kernel, out_shape, specs, scratches, *operands, limit=VMEM_LIMIT):
        return pl.pallas_call(
            kernel, out_shape=out_shape, in_specs=specs,
            out_specs=jax.tree.map(lambda _: VMEM, out_shape), scratch_shapes=scratches,
            compiler_params=pltpu.CompilerParams(vmem_limit_bytes=limit),
        )(*operands)

    def send(x, to):
        pairs = []
        for r in range(nrow):
            for c in range(ncol):
                nr, nc = to(r, c)
                pairs.append((r * ncol + c, (nr % nrow) * ncol + nc))
        return lax.ppermute(x, ("row", "col"), pairs)

    def partner(x):
        return send(x, lambda r, c: (r, c ^ 1))

    def across(x):
        return send(x, lambda r, c: (r, c ^ 2))

    def outward(x, d=0):
        return send(x, lambda r, c: (r + (1 if c % 2 == 0 else -1), c ^ d))

    cols = block_cols.T
    null_mine = outward(near_null)
    cols_mine = outward(cols)
    packed = call(
        pack_kernel, array((rows, size, 2 * slots * size), bf16), [HBM],
        [scratch(weights.shape, f32), pltpu.SemaphoreType.DMA((CHUNKS if rows % CHUNKS == 0 else 1,))],
        weights, limit=PACK_LIMIT)
    targets = call(
        functools.partial(aim_kernel, all_rows), array((total, rows), i32), [VMEM] * 2, [],
        counts.reshape(1, rows), cols)
    null_other = partner(null_mine)
    cols_other = partner(cols_mine)
    count = (slots // 2) * rows + -(-rows // 16) * 8
    block, unit = call(
        functools.partial(unit_kernel, size),
        [array((count, LANES), f32), array((3 * rows + 8, LANES), f32)],
        [SMEM] + [VMEM] * 5, [scratch((8 * rows, size), f32)],
        targets, null_mine, null_other, near_null, prior_ridge, packed)
    hots = call(
        functools.partial(hot_kernel, slots, all_rows),
        [array((3 * rows + 1, total, LANES), bf16)] * 2 + [array((3 * rows, rows * total), bf16)],
        [VMEM] * 3,
        [scratch((3 * rows * total, LANES), f32)] * 2 + [scratch((rows * total, LANES), f32)],
        cols_mine, cols_other, cols)
    own = jnp.concatenate([block, partner(block)])
    diagonal = outward(own, 2)
    straight = outward(own)
    far = across(block)
    far_partner = partner(far)
    last = partner(jnp.concatenate([straight, diagonal]))
    ready = call(
        functools.partial(ready_kernel, size, slots),
        [array((2 * rows, total, LANES), bf16)] * 2
        + [array((rows, 2 * total, LANES), bf16), array((rows, total, LANES), bf16)],
        [VMEM] * 6, [scratch((rows * total, LANES), f32)],
        straight, diagonal, own, far, far_partner, unit)
    parts = call(
        functools.partial(coarse_kernel, size, ncol, nrow),
        array((nrow * ncol, rows // ncol, LANES), f32), [SMEM] + [VMEM] * 10,
        [
            scratch((rows * total // 2, LANES), f32),
            scratch((3 * rows + 1, total, LANES), bf16),
            scratch((3 * rows + 1, total, LANES), bf16),
            scratch((rows, (slots + 1) * total, LANES), bf16),
            scratch((rows, 2 * total, (slots + 1) * total), bf16),
            scratch((rows * total, 2 * LANES), bf16),
        ],
        targets, last, unit, *ready, *hots, packed)
    got = lax.all_to_all(parts, ("row", "col"), 0, 0)
    return call(
        functools.partial(sum_kernel, ncol, nrow), array((rows // ncol, LANES), f32), [VMEM], [], got)


def solution(mesh):
    placed = (P("row", "col", None, None), P("row", None), P("row"), P("row", None), P("row", None))

    return jax.shard_map(on_device, mesh=mesh, in_specs=placed, out_specs=P(("row", "col"), None), check_vma=False)
```

```python
import functools

import jax
import jax.numpy as jnp
from jax import lax
from jax.experimental import pallas as pl
from jax.experimental.pallas import tpu as pltpu
from jax.sharding import PartitionSpec as P


H = 21
BAND = 128
LANES = 128

epsilon = 1e-06
relax_weight = 2.0 / 3.0

NT = (((1,), (1,)), ((), ()))
NN = (((1,), (0,)), ((), ()))


def mxu(a, b, dims):
    return lax.dot_general(a, b, dims, preferred_element_type=jnp.float32)


def split(x):
    hi = x.astype(jnp.bfloat16)
    lo = (x - hi.astype(jnp.float32)).astype(jnp.bfloat16)
    return hi, lo


def lane_iota(shape):
    return lax.broadcasted_iota(jnp.int32, shape, len(shape) - 1)


def row_iota(shape):
    return lax.broadcasted_iota(jnp.int32, shape, 0)


def wrap(x, count):
    x = jnp.where(x < 0, x + count, x)
    return jnp.where(x >= count, x - count, x)


def roll(x, by):
    return pltpu.roll(x, by % LANES, 1)


def pack_kernel(w_hbm, pack_ref, w_ref, sems):
    rows, slots, size, _ = w_ref.shape
    per = LANES // size
    chunks = sems.shape[0]
    step = rows // chunks
    copies = [
        pltpu.make_async_copy(w_hbm.at[pl.ds(n * step, step)], w_ref.at[pl.ds(n * step, step)], sems.at[n])
        for n in range(chunks)
    ]
    for copy in copies:
        copy.start()
    for i in range(rows):
        if i % step == 0:
            copies[i // step].wait()
        for p in range(slots // per):
            tile = jnp.concatenate([w_ref[i, per * p + h] for h in range(per)], axis=1)
            hi, lo = split(tile)
            pack_ref[i, :, 2 * p * LANES : (2 * p + 1) * LANES] = hi
            pack_ref[i, :, (2 * p + 1) * LANES : 2 * (p + 1) * LANES] = lo


def two_part(hi, lo):
    top = jnp.concatenate([hi, hi], axis=1)
    return jnp.concatenate([top, jnp.concatenate([lo, jnp.zeros_like(lo)], axis=1)], axis=0)


def aim(all_rows, counts, cols):
    total, rows = cols.shape
    local = lane_iota((total, rows))
    first = lax.axis_index("row") * rows
    at = wrap(cols - (first + local) + H, all_rows) + (rows - H) + local
    mirror = jnp.where(at < rows, at + 2 * rows, jnp.where(at >= 2 * rows, at - 2 * rows, at))
    at = jnp.where(lax.axis_index("col") % 2 == 0, at, mirror)
    return jnp.where(row_iota((total, rows)) < counts[None, :], at, 3 * rows)


def unit_kernel(size, targets, mine_ref, other_ref, own_ref, ridge_ref, pack_ref,
                block_ref, unit_ref, acc_ref, one_ref):
    rows = own_ref.shape[0]
    slots = pack_ref.shape[2] // (2 * size)
    column = lax.axis_index("col")
    for g, ref in enumerate((mine_ref, own_ref, other_ref)):
        x = ref[...]
        unit = x / jnp.sqrt(jnp.sum(x * x, axis=1, keepdims=True) + epsilon)
        unit_ref[g * rows : (g + 1) * rows, :] = jnp.concatenate([unit, unit], axis=1)
    unit_ref[3 * rows :, :] = jnp.zeros((8, LANES), jnp.float32)
    one_ref[: 3 * rows, :] = jnp.ones((3 * rows, LANES), jnp.float32)
    one_ref[3 * rows :, :] = jnp.zeros((8, LANES), jnp.float32)
    row8 = row_iota((8, LANES))
    half = lane_iota((8, LANES)) // size
    for i in range(rows):
        both = None
        for p in range(slots // 2):
            tile = jnp.zeros((8, LANES), jnp.float32)
            for h in range(2):
                k = 2 * p + h
                t = targets[column * slots + k, i]
                vec = jnp.broadcast_to(unit_ref[pl.ds(t, 1), :], (8, LANES))
                one = jnp.broadcast_to(one_ref[pl.ds(t, 1), :], (8, LANES))
                tile = jnp.where((row8 == k) & (half == h), vec, tile)
                tile = jnp.where((row8 == slots) & (half == h), one, tile)
            term = mxu(two_part(*split(tile)), pack_ref[i, :, 2 * p * LANES : 2 * (p + 1) * LANES], NT)
            both = term if both is None else both + term
        acc_ref[8 * i : 8 * i + 8, :] = both[:8] + both[8:]
    plane = [acc_ref[pl.ds(k, rows, stride=8), :] for k in range(slots + 1)]
    for p in range(slots // 2):
        block_ref[p * rows : (p + 1) * rows, :] = jnp.concatenate(plane[2 * p : 2 * p + 2], axis=1)
    degree = plane[slots] + jnp.where(column == 0, ridge_ref[...], 0.0)
    keep = block_ref.shape[0] - (slots // 2) * rows
    rest = jnp.concatenate([degree[keep:], jnp.zeros((2 * keep - rows, size), jnp.float32)], axis=0)
    block_ref[(slots // 2) * rows :, :] = jnp.concatenate([degree[:keep], rest], axis=1)


def hot_kernel(slots, all_rows, mine_ref, other_ref, own_ref, even_ref, odd_ref, turned_ref,
               even_tmp, odd_tmp, turn_tmp):
    total, rows = own_ref.shape
    column = lax.axis_index("col")
    reach = jnp.where(column % 2 == 0, rows, -rows)
    lane = lane_iota((rows, LANES))
    pairs = total // 2
    for g, ref in enumerate((mine_ref, own_ref, other_ref)):
        cols = ref[...]
        local = row_iota((rows, LANES)) + (g - 1) * reach
        cols = jnp.concatenate([cols, jnp.zeros((total, LANES - rows), jnp.int32)], axis=1)
        cols = jnp.concatenate([cols, jnp.zeros((LANES - total, LANES), jnp.int32)], axis=0)
        cols = cols.T[:rows]
        base = lax.axis_index("row") * rows + local
        where = wrap(wrap(cols - base + H, all_rows), all_rows) - H + local + 2 * rows
        bit = slots
        while bit < total:
            swapped = jnp.where((lane // bit) % 2 == 1, roll(where, bit), roll(where, -bit))
            where = jnp.where((column * slots // bit) % 2 == 1, swapped, where)
            bit *= 2
        for s in range(total):
            spread = jnp.broadcast_to(where[:, s : s + 1], (rows, LANES))
            hot = jnp.where(spread == lane, 1.0, 0.0)
            at, other = s // 2 + (s % 2) * pairs, s // 2 + (1 - s % 2) * pairs
            even_tmp[pl.ds(g * rows * total + at, rows, stride=total), :] = hot
            odd_tmp[pl.ds(g * rows * total + other, rows, stride=total), :] = hot
            if g == 1:
                turn_tmp[pl.ds(at, rows, stride=total), :] = jnp.where(
                    spread == LANES - 1 - lane, 1.0, 0.0)
    for j in range(3 * rows):
        even_ref[j] = even_tmp[j * total : (j + 1) * total, :].astype(jnp.bfloat16)
        odd_ref[j] = odd_tmp[j * total : (j + 1) * total, :].astype(jnp.bfloat16)
    even_ref[3 * rows] = jnp.zeros((total, LANES), jnp.bfloat16)
    odd_ref[3 * rows] = jnp.zeros((total, LANES), jnp.bfloat16)
    for n in range(rows * total // LANES):
        lanes = slice(n * LANES, (n + 1) * LANES)
        turned = turn_tmp[lanes, :].T
        turned_ref[:, lanes] = turned[LANES - 4 * rows : LANES - rows].astype(jnp.bfloat16)


def prolong_rows(planes, unit, column, slots, size, p_ref, first, store):
    rows, ncol = unit.shape[0], len(planes)
    pairs = slots // 2
    half = pairs * ncol
    low_half = lane_iota((rows, LANES)) < size
    degree = sum(block(pairs * rows, None) for block in planes)
    keep = degree.shape[0]
    degree = jnp.concatenate([degree, roll(degree, size)[: rows - keep]], axis=0)
    inverse = relax_weight / jnp.where(low_half, degree, 1.0)
    inverse = jnp.where(low_half, inverse, roll(inverse, size))
    own_term = jnp.where(low_half, (1.0 - relax_weight) * unit, 0.0)
    for d in range(ncol):
        for p in range(pairs):
            v = planes[d](p * rows, (p + 1) * rows) * inverse
            if p == 0:
                v = v + jnp.where(column == d, own_term, 0.0)
            p_ref[pl.ds(first * half + d * pairs + p, rows, stride=half), :] = v
    for j in range(first, first + rows):
        v = p_ref[j * half : (j + 1) * half, :]
        store(j, jnp.concatenate([v, roll(v, size)], axis=0))


def block_of(ref, index, size):
    def rows_of(start, stop):
        return ref[index * size + start : index * size + (size if stop is None else stop), :]

    return rows_of


def ready_kernel(size, slots, straight_ref, diagonal_ref, own_ref, far_ref, far_partner_ref, unit_ref,
                 qh_ref, ql_ref, left_ref, diagonal_term_ref, p_ref):
    count = far_ref.shape[0]
    rows, total, _ = diagonal_term_ref.shape
    column = lax.axis_index("col")
    degree = own_ref[(slots // 2) * rows : count, :]
    degree = jnp.concatenate([degree, roll(degree, size)[: rows - degree.shape[0]]], axis=0)
    low_half = lane_iota((total, LANES)) < size
    groups = (
        [(straight_ref, 0), (straight_ref, 1), (diagonal_ref, 0), (diagonal_ref, 1)],
        [(own_ref, 0), (own_ref, 1), (far_ref, 0), (far_partner_ref, 0)],
    )

    def store(j, q):
        qh_ref[j], ql_ref[j] = split(q)
        if j >= rows:
            i = j - rows
            hi, lo = split(jnp.where(low_half, q, roll(q, size)))
            left_ref[i, :total, :] = hi
            left_ref[i, total:, :] = jnp.where(low_half, lo, jnp.zeros_like(lo))
            term = q[:, :size] * degree[i : i + 1, :size]
            diagonal_term_ref[i] = jnp.concatenate(split(term), axis=1)

    for g, group in enumerate(groups):
        blocks = [block_of(ref, index, count) for ref, index in group]
        unit = unit_ref[g * rows : (g + 1) * rows, :]
        prolong_rows(blocks, unit, column, slots, size, p_ref, g * rows, store)


def coarse_kernel(size, ncol, nrow, targets, last_ref, unit_ref, ready_h_ref, ready_l_ref, left_ref,
                  diagonal_term_ref, even_ref, odd_ref, turned_ref, pack_ref, out_ref,
                  p_ref, qh_ref, ql_ref, r_ref, s_ref, t_ref):
    rows = pack_ref.shape[0]
    slots = pack_ref.shape[2] // (2 * size)
    total = slots * ncol
    pairs = slots // 2
    column = lax.axis_index("col")
    count = last_ref.shape[0] // ncol

    def store(j, q):
        qh_ref[2 * rows + j], ql_ref[2 * rows + j] = split(q)

    blocks = [block_of(last_ref, d ^ 1, count) for d in range(ncol)]
    prolong_rows(blocks, unit_ref[2 * rows : 3 * rows, :], column, slots, size, p_ref, 0, store)
    for table, ready in ((qh_ref, ready_h_ref), (ql_ref, ready_l_ref)):
        table[: 2 * rows] = ready[...]
        table[3 * rows] = jnp.zeros((total, LANES), jnp.bfloat16)
    tile_half = lane_iota((total, LANES)) // size
    zero = jnp.zeros((total, LANES), jnp.bfloat16)
    tiles = [[targets[column * slots + k, i] for k in range(slots)] for i in range(rows)]
    for i in range(rows):
        for p in range(pairs):
            his, los = [], []
            for h in range(2):
                t = tiles[i][2 * p + h]
                his.append(jnp.where(tile_half == h, qh_ref[t], zero))
                los.append(jnp.where(tile_half == h, ql_ref[t], zero))
            lhs = two_part(jnp.concatenate(his, axis=0), jnp.concatenate(los, axis=0))
            both = mxu(lhs, pack_ref[i, :, 2 * p * LANES : 2 * (p + 1) * LANES], NT)
            hi, lo = split(both[: 2 * total] + both[2 * total :])
            at = slice(2 * p * total, 2 * (p + 1) * total)
            r_ref[i, at, :] = jnp.concatenate([hi, lo], axis=1)
        r_ref[i, slots * total :, :] = diagonal_term_ref[i]
    sign = jnp.where(lane_iota((total, (slots + 1) * total)) < slots * total, -1.0, 1.0)
    for i in range(rows):
        both = mxu(left_ref[i], r_ref[i], NT)
        s_ref[i, :total, :], s_ref[i, total:, :] = split((both[:total] + both[total:]) * sign)
    for i in range(rows):
        hot = [(even_ref if k % 2 == 0 else odd_ref)[tiles[i][k]] for k in range(slots)]
        both = mxu(s_ref[i], jnp.concatenate(hot + [even_ref[rows + i]], axis=0), NN)
        at = slice(i * total, (i + 1) * total)
        t_ref[at, :LANES], t_ref[at, LANES:] = split(both[:total] + both[total:])
    both = mxu(turned_ref[...], t_ref[...], NN)
    absolute = both[:, :LANES] + both[:, LANES:]
    relative = [
        pltpu.roll(absolute[n : n + 8], (BAND // 2 - 4 * rows + 1 + n) % LANES, 1, stride=1, stride_axis=0)
        for n in range(0, 3 * rows, 8)
    ]
    relative = jnp.concatenate(relative, axis=0)
    share = rows // ncol
    out_ref[...] = jnp.zeros_like(out_ref)
    for g in range(3):
        row = wrap(lax.axis_index("row") + (g - 1), nrow)
        for c in range(ncol):
            at = (3 - g) * rows - (c + 1) * share
            out_ref[row * ncol + c] = relative[at : at + share]


def sum_kernel(ncol, nrow, got_ref, out_ref):
    total = None
    for step in (-1, 0, 1):
        row = wrap(lax.axis_index("row") + step, nrow)
        for c in range(ncol):
            part = got_ref[row * ncol + c]
            total = part if total is None else total + part
    for n in range(total.shape[0]):
        out_ref[n : n + 1, :] = total[total.shape[0] - 1 - n : total.shape[0] - n]


HBM = pl.BlockSpec(memory_space=pltpu.HBM)
SMEM = pl.BlockSpec(memory_space=pltpu.SMEM)
VMEM = pl.BlockSpec(memory_space=pltpu.VMEM)
VMEM_LIMIT = 20 * 1024 * 1024
PACK_LIMIT = 51 * 1024 * 1024
CHUNKS = 6


def on_device(weights, block_cols, counts, near_null, prior_ridge):
    rows, slots, size, _ = weights.shape
    total = block_cols.shape[1]
    nrow, ncol = lax.axis_size("row"), lax.axis_size("col")
    all_rows = rows * nrow
    f32, bf16 = jnp.float32, jnp.bfloat16
    array = jax.ShapeDtypeStruct
    scratch = pltpu.VMEM

    def call(kernel, out_shape, specs, scratches, *operands, limit=VMEM_LIMIT):
        return pl.pallas_call(
            kernel, out_shape=out_shape, in_specs=specs,
            out_specs=jax.tree.map(lambda _: VMEM, out_shape), scratch_shapes=scratches,
            compiler_params=pltpu.CompilerParams(vmem_limit_bytes=limit),
        )(*operands)

    def send(x, to):
        pairs = []
        for r in range(nrow):
            for c in range(ncol):
                nr, nc = to(r, c)
                pairs.append((r * ncol + c, (nr % nrow) * ncol + nc))
        return lax.ppermute(x, ("row", "col"), pairs)

    def partner(x):
        return send(x, lambda r, c: (r, c ^ 1))

    def across(x):
        return send(x, lambda r, c: (r, c ^ 2))

    def outward(x, d=0):
        return send(x, lambda r, c: (r + (1 if c % 2 == 0 else -1), c ^ d))

    cols = block_cols.T
    null_mine = outward(near_null)
    cols_mine = outward(cols)
    packed = call(
        pack_kernel, array((rows, size, 2 * slots * size), bf16), [HBM],
        [scratch(weights.shape, f32), pltpu.SemaphoreType.DMA((CHUNKS if rows % CHUNKS == 0 else 1,))],
        weights, limit=PACK_LIMIT)
    targets = aim(all_rows, counts, cols)
    null_other = partner(null_mine)
    cols_other = partner(cols_mine)
    count = (slots // 2) * rows + -(-rows // 16) * 8
    block, unit = call(
        functools.partial(unit_kernel, size),
        [array((count, LANES), f32), array((3 * rows + 8, LANES), f32)],
        [SMEM] + [VMEM] * 5, [scratch((8 * rows, size), f32), scratch((3 * rows + 8, LANES), f32)],
        targets, null_mine, null_other, near_null, prior_ridge, packed)
    hots = call(
        functools.partial(hot_kernel, slots, all_rows),
        [array((3 * rows + 1, total, LANES), bf16)] * 2 + [array((3 * rows, rows * total), bf16)],
        [VMEM] * 3,
        [scratch((3 * rows * total, LANES), f32)] * 2 + [scratch((rows * total, LANES), f32)],
        cols_mine, cols_other, cols)
    own = jnp.concatenate([block, partner(block)])
    diagonal = outward(own, 2)
    straight = outward(own)
    far = across(block)
    far_partner = partner(far)
    last = partner(jnp.concatenate([straight, diagonal]))
    ready = call(
        functools.partial(ready_kernel, size, slots),
        [array((2 * rows, total, LANES), bf16)] * 2
        + [array((rows, 2 * total, LANES), bf16), array((rows, total, LANES), bf16)],
        [VMEM] * 6, [scratch((rows * total, LANES), f32)],
        straight, diagonal, own, far, far_partner, unit)
    parts = call(
        functools.partial(coarse_kernel, size, ncol, nrow),
        array((nrow * ncol, rows // ncol, LANES), f32), [SMEM] + [VMEM] * 10,
        [
            scratch((rows * total // 2, LANES), f32),
            scratch((3 * rows + 1, total, LANES), bf16),
            scratch((3 * rows + 1, total, LANES), bf16),
            scratch((rows, (slots + 1) * total, LANES), bf16),
            scratch((rows, 2 * total, (slots + 1) * total), bf16),
            scratch((rows * total, 2 * LANES), bf16),
        ],
        targets, last, unit, *ready, *hots, packed)
    got = lax.all_to_all(parts, ("row", "col"), 0, 0)
    return call(
        functools.partial(sum_kernel, ncol, nrow), array((rows // ncol, LANES), f32), [VMEM], [], got)


def solution(mesh):
    placed = (P("row", "col", None, None), P("row", None), P("row"), P("row", None), P("row", None))

    return jax.shard_map(on_device, mesh=mesh, in_specs=placed, out_specs=P(("row", "col"), None), check_vma=False)
```

```python
import functools

import jax
import jax.numpy as jnp
from jax import lax
from jax.experimental import pallas as pl
from jax.experimental.pallas import tpu as pltpu
from jax.sharding import PartitionSpec as P


H = 21
BAND = 128
LANES = 128

epsilon = 1e-06
relax_weight = 2.0 / 3.0

NT = (((1,), (1,)), ((), ()))
NN = (((1,), (0,)), ((), ()))


def mxu(a, b, dims):
    return lax.dot_general(a, b, dims, preferred_element_type=jnp.float32)


def split(x):
    hi = x.astype(jnp.bfloat16)
    lo = (x - hi.astype(jnp.float32)).astype(jnp.bfloat16)
    return hi, lo


def lane_iota(shape):
    return lax.broadcasted_iota(jnp.int32, shape, len(shape) - 1)


def row_iota(shape):
    return lax.broadcasted_iota(jnp.int32, shape, 0)


def wrap(x, count):
    x = jnp.where(x < 0, x + count, x)
    return jnp.where(x >= count, x - count, x)


def roll(x, by):
    return pltpu.roll(x, by % LANES, 1)


def pack_kernel(w_hbm, pack_ref, w_ref, sems):
    rows, slots, size, _ = w_ref.shape
    per = LANES // size
    chunks = sems.shape[0]
    step = rows // chunks
    copies = [
        pltpu.make_async_copy(w_hbm.at[pl.ds(n * step, step)], w_ref.at[pl.ds(n * step, step)], sems.at[n])
        for n in range(chunks)
    ]
    for copy in copies:
        copy.start()
    for i in range(rows):
        if i % step == 0:
            copies[i // step].wait()
        for p in range(slots // per):
            tile = jnp.concatenate([w_ref[i, per * p + h] for h in range(per)], axis=1)
            hi, lo = split(tile)
            pack_ref[i, :, 2 * p * LANES : (2 * p + 1) * LANES] = hi
            pack_ref[i, :, (2 * p + 1) * LANES : 2 * (p + 1) * LANES] = lo


def two_part(hi, lo):
    top = jnp.concatenate([hi, hi], axis=1)
    return jnp.concatenate([top, jnp.concatenate([lo, jnp.zeros_like(lo)], axis=1)], axis=0)


def aim(all_rows, counts, cols):
    total, rows = cols.shape
    local = lane_iota((total, rows))
    first = lax.axis_index("row") * rows
    at = wrap(cols - (first + local) + H, all_rows) + (rows - H) + local
    mirror = jnp.where(at < rows, at + 2 * rows, jnp.where(at >= 2 * rows, at - 2 * rows, at))
    at = jnp.where(lax.axis_index("col") % 2 == 0, at, mirror)
    return jnp.where(row_iota((total, rows)) < counts[None, :], at, 3 * rows)


def unit_kernel(size, targets, mine_ref, other_ref, own_ref, ridge_ref, pack_ref,
                block_ref, unit_ref, acc_ref, one_ref):
    rows = own_ref.shape[0]
    slots = pack_ref.shape[2] // (2 * size)
    column = lax.axis_index("col")
    for g, ref in enumerate((mine_ref, own_ref, other_ref)):
        x = ref[...]
        unit = x / jnp.sqrt(jnp.sum(x * x, axis=1, keepdims=True) + epsilon)
        unit_ref[g * rows : (g + 1) * rows, :] = jnp.concatenate([unit, unit], axis=1)
    unit_ref[3 * rows :, :] = jnp.zeros((8, LANES), jnp.float32)
    one_ref[: 3 * rows, :] = jnp.ones((3 * rows, LANES), jnp.float32)
    one_ref[3 * rows :, :] = jnp.zeros((8, LANES), jnp.float32)
    row8 = row_iota((8, LANES))
    half = lane_iota((8, LANES)) // size
    for i in range(rows):
        both = None
        for p in range(slots // 2):
            tile = jnp.zeros((8, LANES), jnp.float32)
            for h in range(2):
                k = 2 * p + h
                t = targets[column * slots + k, i]
                vec = jnp.broadcast_to(unit_ref[pl.ds(t, 1), :], (8, LANES))
                one = jnp.broadcast_to(one_ref[pl.ds(t, 1), :], (8, LANES))
                tile = jnp.where((row8 == k) & (half == h), vec, tile)
                tile = jnp.where((row8 == slots) & (half == h), one, tile)
            term = mxu(two_part(*split(tile)), pack_ref[i, :, 2 * p * LANES : 2 * (p + 1) * LANES], NT)
            both = term if both is None else both + term
        acc_ref[8 * i : 8 * i + 8, :] = both[:8] + both[8:]
    plane = [acc_ref[pl.ds(k, rows, stride=8), :] for k in range(slots + 1)]
    for p in range(slots // 2):
        block_ref[p * rows : (p + 1) * rows, :] = jnp.concatenate(plane[2 * p : 2 * p + 2], axis=1)
    degree = plane[slots] + jnp.where(column == 0, ridge_ref[...], 0.0)
    keep = block_ref.shape[0] - (slots // 2) * rows
    rest = jnp.concatenate([degree[keep:], jnp.zeros((2 * keep - rows, size), jnp.float32)], axis=0)
    block_ref[(slots // 2) * rows :, :] = jnp.concatenate([degree[:keep], rest], axis=1)


def hot_kernel(slots, all_rows, mine_ref, other_ref, own_ref, even_ref, odd_ref, turned_ref,
               even_tmp, odd_tmp, turn_tmp):
    total, rows = own_ref.shape
    column = lax.axis_index("col")
    reach = jnp.where(column % 2 == 0, rows, -rows)
    lane = lane_iota((rows, LANES))
    pairs = total // 2
    for g, ref in enumerate((mine_ref, own_ref, other_ref)):
        cols = ref[...]
        local = row_iota((rows, LANES)) + (g - 1) * reach
        cols = jnp.concatenate([cols, jnp.zeros((total, LANES - rows), jnp.int32)], axis=1)
        cols = jnp.concatenate([cols, jnp.zeros((LANES - total, LANES), jnp.int32)], axis=0)
        cols = cols.T[:rows]
        base = lax.axis_index("row") * rows + local
        where = wrap(wrap(cols - base + H, all_rows), all_rows) - H + local + 2 * rows
        bit = slots
        while bit < total:
            swapped = jnp.where((lane // bit) % 2 == 1, roll(where, bit), roll(where, -bit))
            where = jnp.where((column * slots // bit) % 2 == 1, swapped, where)
            bit *= 2
        for s in range(total):
            spread = jnp.broadcast_to(where[:, s : s + 1], (rows, LANES))
            hot = jnp.where(spread == lane, 1.0, 0.0)
            at, other = s // 2 + (s % 2) * pairs, s // 2 + (1 - s % 2) * pairs
            even_tmp[pl.ds(g * rows * total + at, rows, stride=total), :] = hot
            odd_tmp[pl.ds(g * rows * total + other, rows, stride=total), :] = hot
            if g == 1:
                turn_tmp[pl.ds(at, rows, stride=total), :] = jnp.where(
                    spread == LANES - 1 - lane, 1.0, 0.0)
    for j in range(3 * rows):
        even_ref[j] = even_tmp[j * total : (j + 1) * total, :].astype(jnp.bfloat16)
        odd_ref[j] = odd_tmp[j * total : (j + 1) * total, :].astype(jnp.bfloat16)
    even_ref[3 * rows] = jnp.zeros((total, LANES), jnp.bfloat16)
    odd_ref[3 * rows] = jnp.zeros((total, LANES), jnp.bfloat16)
    for n in range(rows * total // LANES):
        lanes = slice(n * LANES, (n + 1) * LANES)
        turned = turn_tmp[lanes, :].T
        turned_ref[:, lanes] = turned[LANES - 4 * rows : LANES - rows].astype(jnp.bfloat16)


def prolong_rows(planes, unit, column, slots, size, p_ref, first, store):
    rows, ncol = unit.shape[0], len(planes)
    pairs = slots // 2
    half = pairs * ncol
    low_half = lane_iota((rows, LANES)) < size
    degree = sum(block(pairs * rows, None) for block in planes)
    keep = degree.shape[0]
    degree = jnp.concatenate([degree, roll(degree, size)[: rows - keep]], axis=0)
    inverse = relax_weight / jnp.where(low_half, degree, 1.0)
    inverse = jnp.where(low_half, inverse, roll(inverse, size))
    own_term = jnp.where(low_half, (1.0 - relax_weight) * unit, 0.0)
    for d in range(ncol):
        for p in range(pairs):
            v = planes[d](p * rows, (p + 1) * rows) * inverse
            if p == 0:
                v = v + jnp.where(column == d, own_term, 0.0)
            p_ref[pl.ds(first * half + d * pairs + p, rows, stride=half), :] = v
    for j in range(first, first + rows):
        v = p_ref[j * half : (j + 1) * half, :]
        store(j, jnp.concatenate([v, roll(v, size)], axis=0))


def block_of(ref, index, size):
    def rows_of(start, stop):
        return ref[index * size + start : index * size + (size if stop is None else stop), :]

    return rows_of


def own_kernel(size, own_ref, far_ref, far_partner_ref, unit_ref, pack_ref,
               qh_ref, ql_ref, v_ref, diagonal_ref, p_ref):
    rows, total, _ = qh_ref.shape
    slots = pack_ref.shape[2] // (2 * size)
    count = far_ref.shape[0]
    degree = own_ref[(slots // 2) * rows : count, :]
    degree = jnp.concatenate([degree, roll(degree, size)[: rows - degree.shape[0]]], axis=0)
    low_half = lane_iota((total, LANES)) < size
    kept = []

    def store(i, q):
        hi, lo = split(q)
        qh_ref[i], ql_ref[i] = hi, lo
        term = q[:, :size] * degree[i : i + 1, :size]
        kept.append((jnp.concatenate([hi[:, :size], lo[:, :size]], axis=0),
                     jnp.where(low_half, q, roll(q, size)), jnp.concatenate(split(term), axis=1)))

    group = [(own_ref, 0), (own_ref, 1), (far_ref, 0), (far_partner_ref, 0)]
    blocks = [block_of(ref, index, count) for ref, index in group]
    prolong_rows(blocks, unit_ref[rows : 2 * rows, :], lax.axis_index("col"), slots, size, p_ref, 0, store)
    for i, (left, _, _) in enumerate(kept):
        both = mxu(left, pack_ref[i], NN)
        for p in range(slots // 2):
            at = 2 * p * LANES
            hi_lanes, lo_lanes = slice(at, at + LANES), slice(at + LANES, at + 2 * LANES)
            v = both[:total, hi_lanes] + both[:total, lo_lanes] + both[total:, hi_lanes]
            v_ref[i, :, at : at + 2 * LANES] = two_part(*split(-v))
    for i, (_, doubled, term) in enumerate(kept):
        hi, lo = split(doubled)
        both = mxu(jnp.concatenate([hi, jnp.where(low_half, lo, jnp.zeros_like(lo))], axis=0), term, NT)
        diagonal_ref[i] = jnp.concatenate(split(both[:total] + both[total:]), axis=0)


def ready_kernel(size, slots, straight_ref, diagonal_ref, unit_ref, qh_ref, ql_ref, p_ref):
    rows = qh_ref.shape[0]
    count = straight_ref.shape[0] // 2

    def store(j, q):
        qh_ref[j], ql_ref[j] = split(q)

    blocks = [block_of(ref, index, count) for ref in (straight_ref, diagonal_ref) for index in range(2)]
    prolong_rows(blocks, unit_ref[:rows, :], lax.axis_index("col"), slots, size, p_ref, 0, store)


def coarse_kernel(size, slots, ncol, nrow, targets, last_ref, unit_ref, own_h_ref, own_l_ref, v_ref,
                  diagonal_ref, mine_h_ref, mine_l_ref, even_ref, odd_ref, turned_ref, out_ref,
                  p_ref, qh_ref, ql_ref, s_ref, t_ref):
    rows, total, _ = own_h_ref.shape
    pairs = slots // 2
    column = lax.axis_index("col")
    count = last_ref.shape[0] // ncol

    def store(j, q):
        qh_ref[2 * rows + j], ql_ref[2 * rows + j] = split(q)

    blocks = [block_of(last_ref, d ^ 1, count) for d in range(ncol)]
    prolong_rows(blocks, unit_ref[2 * rows : 3 * rows, :], column, slots, size, p_ref, 0, store)
    for table, mine, own in ((qh_ref, mine_h_ref, own_h_ref), (ql_ref, mine_l_ref, own_l_ref)):
        table[:rows] = mine[...]
        table[rows : 2 * rows] = own[...]
        table[3 * rows] = jnp.zeros((total, LANES), jnp.bfloat16)
    tile_half = lane_iota((total, LANES)) // size
    zero = jnp.zeros((total, LANES), jnp.bfloat16)
    tiles = [[targets[column * slots + k, i] for k in range(slots)] for i in range(rows)]
    for i in range(rows):
        for p in range(pairs):
            right = []
            for h in range(2):
                t = tiles[i][2 * p + h]
                parts = [jnp.where(tile_half == h, table[t], zero) for table in (qh_ref, ql_ref)]
                right.append(jnp.concatenate(parts, axis=1))
            both = mxu(v_ref[i, :, 2 * p * LANES : 2 * (p + 1) * LANES], jnp.concatenate(right, axis=0), NT)
            at = slice(2 * p * total, 2 * (p + 1) * total)
            s_ref[i, :total, at], s_ref[i, total:, at] = split(both[:total] + both[total:])
        s_ref[i, :, slots * total :] = diagonal_ref[i]
    for i in range(rows):
        hot = [(even_ref if k % 2 == 0 else odd_ref)[tiles[i][k]] for k in range(slots)]
        both = mxu(s_ref[i], jnp.concatenate(hot + [even_ref[rows + i]], axis=0), NN)
        at = slice(i * total, (i + 1) * total)
        t_ref[at, :LANES], t_ref[at, LANES:] = split(both[:total] + both[total:])
    both = mxu(turned_ref[...], t_ref[...], NN)
    absolute = both[:, :LANES] + both[:, LANES:]
    relative = [
        pltpu.roll(absolute[n : n + 8], (BAND // 2 - 4 * rows + 1 + n) % LANES, 1, stride=1, stride_axis=0)
        for n in range(0, 3 * rows, 8)
    ]
    relative = jnp.concatenate(relative, axis=0)
    share = rows // ncol
    out_ref[...] = jnp.zeros_like(out_ref)
    for g in range(3):
        row = wrap(lax.axis_index("row") + (g - 1), nrow)
        for c in range(ncol):
            at = (3 - g) * rows - (c + 1) * share
            out_ref[row * ncol + c] = relative[at : at + share]


def sum_kernel(ncol, nrow, got_ref, out_ref):
    total = None
    for step in (-1, 0, 1):
        row = wrap(lax.axis_index("row") + step, nrow)
        for c in range(ncol):
            part = got_ref[row * ncol + c]
            total = part if total is None else total + part
    for n in range(total.shape[0]):
        out_ref[n : n + 1, :] = total[total.shape[0] - 1 - n : total.shape[0] - n]


HBM = pl.BlockSpec(memory_space=pltpu.HBM)
SMEM = pl.BlockSpec(memory_space=pltpu.SMEM)
VMEM = pl.BlockSpec(memory_space=pltpu.VMEM)
VMEM_LIMIT = 20 * 1024 * 1024
PACK_LIMIT = 51 * 1024 * 1024
CHUNKS = 6


def on_device(weights, block_cols, counts, near_null, prior_ridge):
    rows, slots, size, _ = weights.shape
    total = block_cols.shape[1]
    nrow, ncol = lax.axis_size("row"), lax.axis_size("col")
    all_rows = rows * nrow
    f32, bf16 = jnp.float32, jnp.bfloat16
    array = jax.ShapeDtypeStruct
    scratch = pltpu.VMEM

    def call(kernel, out_shape, specs, scratches, *operands, limit=VMEM_LIMIT):
        return pl.pallas_call(
            kernel, out_shape=out_shape, in_specs=specs,
            out_specs=jax.tree.map(lambda _: VMEM, out_shape), scratch_shapes=scratches,
            compiler_params=pltpu.CompilerParams(vmem_limit_bytes=limit),
        )(*operands)

    def send(x, to):
        pairs = []
        for r in range(nrow):
            for c in range(ncol):
                nr, nc = to(r, c)
                pairs.append((r * ncol + c, (nr % nrow) * ncol + nc))
        return lax.ppermute(x, ("row", "col"), pairs)

    def partner(x):
        return send(x, lambda r, c: (r, c ^ 1))

    def across(x):
        return send(x, lambda r, c: (r, c ^ 2))

    def outward(x, d=0):
        return send(x, lambda r, c: (r + (1 if c % 2 == 0 else -1), c ^ d))

    cols = block_cols.T
    null_mine = outward(near_null)
    cols_mine = outward(cols)
    packed = call(
        pack_kernel, array((rows, size, 2 * slots * size), bf16), [HBM],
        [scratch(weights.shape, f32), pltpu.SemaphoreType.DMA((CHUNKS if rows % CHUNKS == 0 else 1,))],
        weights, limit=PACK_LIMIT)
    targets = aim(all_rows, counts, cols)
    null_other = partner(null_mine)
    cols_other = partner(cols_mine)
    count = (slots // 2) * rows + -(-rows // 16) * 8
    block, unit = call(
        functools.partial(unit_kernel, size),
        [array((count, LANES), f32), array((3 * rows + 8, LANES), f32)],
        [SMEM] + [VMEM] * 5, [scratch((8 * rows, size), f32), scratch((3 * rows + 8, LANES), f32)],
        targets, null_mine, null_other, near_null, prior_ridge, packed)
    hots = call(
        functools.partial(hot_kernel, slots, all_rows),
        [array((3 * rows + 1, total, LANES), bf16)] * 2 + [array((3 * rows, rows * total), bf16)],
        [VMEM] * 3,
        [scratch((3 * rows * total, LANES), f32)] * 2 + [scratch((rows * total, LANES), f32)],
        cols_mine, cols_other, cols)
    own = jnp.concatenate([block, partner(block)])
    diagonal = outward(own, 2)
    straight = outward(own)
    far = across(block)
    far_partner = partner(far)
    last = partner(jnp.concatenate([straight, diagonal]))
    own_parts = call(
        functools.partial(own_kernel, size),
        [array((rows, total, LANES), bf16)] * 2
        + [array((rows, 2 * total, 2 * slots * size), bf16), array((rows, 2 * total, total), bf16)],
        [VMEM] * 5, [scratch((rows * total // 2, LANES), f32)],
        own, far, far_partner, unit, packed)
    ready = call(
        functools.partial(ready_kernel, size, slots), [array((rows, total, LANES), bf16)] * 2,
        [VMEM] * 3, [scratch((rows * total // 2, LANES), f32)],
        straight, diagonal, unit)
    parts = call(
        functools.partial(coarse_kernel, size, slots, ncol, nrow),
        array((nrow * ncol, rows // ncol, LANES), f32), [SMEM] + [VMEM] * 11,
        [
            scratch((rows * total // 2, LANES), f32),
            scratch((3 * rows + 1, total, LANES), bf16),
            scratch((3 * rows + 1, total, LANES), bf16),
            scratch((rows, 2 * total, (slots + 1) * total), bf16),
            scratch((rows * total, 2 * LANES), bf16),
        ],
        targets, last, unit, *own_parts, *ready, *hots)
    got = lax.all_to_all(parts, ("row", "col"), 0, 0)
    return call(
        functools.partial(sum_kernel, ncol, nrow), array((rows // ncol, LANES), f32), [VMEM], [], got)


def solution(mesh):
    placed = (P("row", "col", None, None), P("row", None), P("row"), P("row", None), P("row", None))

    return jax.shard_map(on_device, mesh=mesh, in_specs=placed, out_specs=P(("row", "col"), None), check_vma=False)
```

```python
import functools

import jax
import jax.numpy as jnp
from jax import lax
from jax.experimental import pallas as pl
from jax.experimental.pallas import tpu as pltpu
from jax.sharding import PartitionSpec as P


H = 21
BAND = 128
LANES = 128

epsilon = 1e-06
relax_weight = 2.0 / 3.0

NT = (((1,), (1,)), ((), ()))
NN = (((1,), (0,)), ((), ()))


def mxu(a, b, dims):
    return lax.dot_general(a, b, dims, preferred_element_type=jnp.float32)


def split(x):
    hi = x.astype(jnp.bfloat16)
    lo = (x - hi.astype(jnp.float32)).astype(jnp.bfloat16)
    return hi, lo


def lane_iota(shape):
    return lax.broadcasted_iota(jnp.int32, shape, len(shape) - 1)


def row_iota(shape):
    return lax.broadcasted_iota(jnp.int32, shape, 0)


def wrap(x, count):
    x = jnp.where(x < 0, x + count, x)
    return jnp.where(x >= count, x - count, x)


def roll(x, by):
    return pltpu.roll(x, by % LANES, 1)


def pack_kernel(w_hbm, pack_ref, w_ref, sems):
    rows, slots, size, _ = w_ref.shape
    per = LANES // size
    chunks = sems.shape[0]
    step = rows // chunks
    copies = [
        pltpu.make_async_copy(w_hbm.at[pl.ds(n * step, step)], w_ref.at[pl.ds(n * step, step)], sems.at[n])
        for n in range(chunks)
    ]
    for copy in copies:
        copy.start()
    for i in range(rows):
        if i % step == 0:
            copies[i // step].wait()
        for p in range(slots // per):
            tile = jnp.concatenate([w_ref[i, per * p + h] for h in range(per)], axis=1)
            hi, lo = split(tile)
            pack_ref[i, :, 2 * p * LANES : (2 * p + 1) * LANES] = hi
            pack_ref[i, :, (2 * p + 1) * LANES : 2 * (p + 1) * LANES] = lo


def two_part(hi, lo):
    top = jnp.concatenate([hi, hi], axis=1)
    return jnp.concatenate([top, jnp.concatenate([lo, jnp.zeros_like(lo)], axis=1)], axis=0)


def aim(all_rows, start, counts, cols):
    slots, rows = cols.shape
    local = lane_iota((slots, rows))
    first = lax.axis_index("row") * rows
    at = wrap(cols - (first + local) + H, all_rows) + (rows - H) + local
    mirror = jnp.where(at < rows, at + 2 * rows, jnp.where(at >= 2 * rows, at - 2 * rows, at))
    at = jnp.where(lax.axis_index("col") % 2 == 0, at, mirror)
    return jnp.where(row_iota((slots, rows)) + start < counts[None, :], at, 3 * rows)


def unit_kernel(size, targets, mine_ref, other_ref, own_ref, ridge_ref, pack_ref,
                block_ref, unit_ref, acc_ref, one_ref):
    rows = own_ref.shape[0]
    slots = pack_ref.shape[2] // (2 * size)
    column = lax.axis_index("col")
    for g, ref in enumerate((mine_ref, own_ref, other_ref)):
        x = ref[...]
        unit = x / jnp.sqrt(jnp.sum(x * x, axis=1, keepdims=True) + epsilon)
        unit_ref[g * rows : (g + 1) * rows, :] = jnp.concatenate([unit, unit], axis=1)
    unit_ref[3 * rows :, :] = jnp.zeros((8, LANES), jnp.float32)
    one_ref[: 3 * rows, :] = jnp.ones((3 * rows, LANES), jnp.float32)
    one_ref[3 * rows :, :] = jnp.zeros((8, LANES), jnp.float32)
    row8 = row_iota((8, LANES))
    half = lane_iota((8, LANES)) // size
    for i in range(rows):
        both = None
        for p in range(slots // 2):
            tile = jnp.zeros((8, LANES), jnp.float32)
            for h in range(2):
                k = 2 * p + h
                t = targets[k, i]
                vec = jnp.broadcast_to(unit_ref[pl.ds(t, 1), :], (8, LANES))
                one = jnp.broadcast_to(one_ref[pl.ds(t, 1), :], (8, LANES))
                tile = jnp.where((row8 == k) & (half == h), vec, tile)
                tile = jnp.where((row8 == slots) & (half == h), one, tile)
            term = mxu(two_part(*split(tile)), pack_ref[i, :, 2 * p * LANES : 2 * (p + 1) * LANES], NT)
            both = term if both is None else both + term
        acc_ref[8 * i : 8 * i + 8, :] = both[:8] + both[8:]
    plane = [acc_ref[pl.ds(k, rows, stride=8), :] for k in range(slots + 1)]
    for p in range(slots // 2):
        block_ref[p * rows : (p + 1) * rows, :] = jnp.concatenate(plane[2 * p : 2 * p + 2], axis=1)
    degree = plane[slots] + jnp.where(column == 0, ridge_ref[...], 0.0)
    keep = block_ref.shape[0] - (slots // 2) * rows
    rest = jnp.concatenate([degree[keep:], jnp.zeros((2 * keep - rows, size), jnp.float32)], axis=0)
    block_ref[(slots // 2) * rows :, :] = jnp.concatenate([degree[:keep], rest], axis=1)


def hot_kernel(slots, all_rows, mine_ref, other_ref, own_ref, even_ref, odd_ref, turned_ref,
               even_tmp, odd_tmp, turn_tmp):
    total, rows = own_ref.shape
    column = lax.axis_index("col")
    reach = jnp.where(column % 2 == 0, rows, -rows)
    lane = lane_iota((rows, LANES))
    pairs = total // 2
    for g, ref in enumerate((mine_ref, own_ref, other_ref)):
        cols = ref[...]
        local = row_iota((rows, LANES)) + (g - 1) * reach
        cols = jnp.concatenate([cols, jnp.zeros((total, LANES - rows), jnp.int32)], axis=1)
        cols = jnp.concatenate([cols, jnp.zeros((LANES - total, LANES), jnp.int32)], axis=0)
        cols = cols.T[:rows]
        base = lax.axis_index("row") * rows + local
        where = wrap(wrap(cols - base + H, all_rows), all_rows) - H + local + 2 * rows
        bit = slots
        while bit < total:
            swapped = jnp.where((lane // bit) % 2 == 1, roll(where, bit), roll(where, -bit))
            where = jnp.where((column * slots // bit) % 2 == 1, swapped, where)
            bit *= 2
        for s in range(total):
            spread = jnp.broadcast_to(where[:, s : s + 1], (rows, LANES))
            hot = jnp.where(spread == lane, 1.0, 0.0)
            at, other = s // 2 + (s % 2) * pairs, s // 2 + (1 - s % 2) * pairs
            even_tmp[pl.ds(g * rows * total + at, rows, stride=total), :] = hot
            odd_tmp[pl.ds(g * rows * total + other, rows, stride=total), :] = hot
            if g == 1:
                turn_tmp[pl.ds(at, rows, stride=total), :] = jnp.where(
                    spread == LANES - 1 - lane, 1.0, 0.0)
    for j in range(3 * rows):
        even_ref[j] = even_tmp[j * total : (j + 1) * total, :].astype(jnp.bfloat16)
        odd_ref[j] = odd_tmp[j * total : (j + 1) * total, :].astype(jnp.bfloat16)
    even_ref[3 * rows] = jnp.zeros((total, LANES), jnp.bfloat16)
    odd_ref[3 * rows] = jnp.zeros((total, LANES), jnp.bfloat16)
    for n in range(rows * total // LANES):
        lanes = slice(n * LANES, (n + 1) * LANES)
        turned = turn_tmp[lanes, :].T
        turned_ref[:, lanes] = turned[LANES - 4 * rows : LANES - rows].astype(jnp.bfloat16)


def prolong_rows(planes, unit, column, slots, size, p_ref, first, store):
    rows, ncol = unit.shape[0], len(planes)
    pairs = slots // 2
    half = pairs * ncol
    low_half = lane_iota((rows, LANES)) < size
    degree = sum(block(pairs * rows, None) for block in planes)
    keep = degree.shape[0]
    degree = jnp.concatenate([degree, roll(degree, size)[: rows - keep]], axis=0)
    inverse = relax_weight / jnp.where(low_half, degree, 1.0)
    inverse = jnp.where(low_half, inverse, roll(inverse, size))
    own_term = jnp.where(low_half, (1.0 - relax_weight) * unit, 0.0)
    for d in range(ncol):
        for p in range(pairs):
            v = planes[d](p * rows, (p + 1) * rows) * inverse
            if p == 0:
                v = v + jnp.where(column == d, own_term, 0.0)
            p_ref[pl.ds(first * half + d * pairs + p, rows, stride=half), :] = v
    for j in range(first, first + rows):
        v = p_ref[j * half : (j + 1) * half, :]
        store(j, jnp.concatenate([v, roll(v, size)], axis=0))


def block_of(ref, index, size):
    def rows_of(start, stop):
        return ref[index * size + start : index * size + (size if stop is None else stop), :]

    return rows_of


def own_kernel(size, own_ref, far_ref, far_partner_ref, unit_ref, pack_ref,
               qh_ref, ql_ref, v_ref, diagonal_ref, p_ref):
    rows, total, _ = qh_ref.shape
    slots = pack_ref.shape[2] // (2 * size)
    count = far_ref.shape[0]
    degree = own_ref[(slots // 2) * rows : count, :]
    degree = jnp.concatenate([degree, roll(degree, size)[: rows - degree.shape[0]]], axis=0)
    low_half = lane_iota((total, LANES)) < size
    kept = []

    def store(i, q):
        hi, lo = split(q)
        qh_ref[i], ql_ref[i] = hi, lo
        term = q[:, :size] * degree[i : i + 1, :size]
        kept.append((jnp.concatenate([hi[:, :size], lo[:, :size]], axis=0),
                     jnp.where(low_half, q, roll(q, size)), jnp.concatenate(split(term), axis=1)))

    group = [(own_ref, 0), (own_ref, 1), (far_ref, 0), (far_partner_ref, 0)]
    blocks = [block_of(ref, index, count) for ref, index in group]
    prolong_rows(blocks, unit_ref[rows : 2 * rows, :], lax.axis_index("col"), slots, size, p_ref, 0, store)
    for i, (left, _, _) in enumerate(kept):
        both = mxu(left, pack_ref[i], NN)
        for p in range(slots // 2):
            at = 2 * p * LANES
            hi_lanes, lo_lanes = slice(at, at + LANES), slice(at + LANES, at + 2 * LANES)
            v = both[:total, hi_lanes] + both[:total, lo_lanes] + both[total:, hi_lanes]
            v_ref[i, :, at : at + 2 * LANES] = two_part(*split(-v))
    for i, (_, doubled, term) in enumerate(kept):
        hi, lo = split(doubled)
        both = mxu(jnp.concatenate([hi, jnp.where(low_half, lo, jnp.zeros_like(lo))], axis=0), term, NT)
        diagonal_ref[i] = jnp.concatenate(split(both[:total] + both[total:]), axis=0)


def ready_kernel(size, slots, straight_ref, diagonal_ref, unit_ref, qh_ref, ql_ref, p_ref):
    rows = qh_ref.shape[0]
    count = straight_ref.shape[0] // 2

    def store(j, q):
        qh_ref[j], ql_ref[j] = split(q)

    blocks = [block_of(ref, index, count) for ref in (straight_ref, diagonal_ref) for index in range(2)]
    prolong_rows(blocks, unit_ref[:rows, :], lax.axis_index("col"), slots, size, p_ref, 0, store)


def coarse_kernel(size, slots, ncol, nrow, targets, last_ref, diagonal_partner_ref, unit_ref, own_h_ref, own_l_ref, v_ref,
                  diagonal_ref, mine_h_ref, mine_l_ref, even_ref, odd_ref, turned_ref, out_ref,
                  p_ref, qh_ref, ql_ref, s_ref, t_ref):
    rows, total, _ = own_h_ref.shape
    pairs = slots // 2
    column = lax.axis_index("col")
    count = last_ref.shape[0] // 2

    def store(j, q):
        qh_ref[2 * rows + j], ql_ref[2 * rows + j] = split(q)

    blocks = [
        block_of(ref, index, count) for ref in (last_ref, diagonal_partner_ref) for index in (1, 0)
    ]
    prolong_rows(blocks, unit_ref[2 * rows : 3 * rows, :], column, slots, size, p_ref, 0, store)
    for table, mine, own in ((qh_ref, mine_h_ref, own_h_ref), (ql_ref, mine_l_ref, own_l_ref)):
        table[:rows] = mine[...]
        table[rows : 2 * rows] = own[...]
        table[3 * rows] = jnp.zeros((total, LANES), jnp.bfloat16)
    tile_half = lane_iota((total, LANES)) // size
    zero = jnp.zeros((total, LANES), jnp.bfloat16)
    tiles = [[targets[k, i] for k in range(slots)] for i in range(rows)]
    for i in range(rows):
        for p in range(pairs):
            right = []
            for h in range(2):
                t = tiles[i][2 * p + h]
                parts = [jnp.where(tile_half == h, table[t], zero) for table in (qh_ref, ql_ref)]
                right.append(jnp.concatenate(parts, axis=1))
            both = mxu(v_ref[i, :, 2 * p * LANES : 2 * (p + 1) * LANES], jnp.concatenate(right, axis=0), NT)
            at = slice(2 * p * total, 2 * (p + 1) * total)
            s_ref[i, :total, at], s_ref[i, total:, at] = split(both[:total] + both[total:])
        s_ref[i, :, slots * total :] = diagonal_ref[i]
    for i in range(rows):
        hot = [(even_ref if k % 2 == 0 else odd_ref)[tiles[i][k]] for k in range(slots)]
        both = mxu(s_ref[i], jnp.concatenate(hot + [even_ref[rows + i]], axis=0), NN)
        at = slice(i * total, (i + 1) * total)
        t_ref[at, :LANES], t_ref[at, LANES:] = split(both[:total] + both[total:])
    both = mxu(turned_ref[...], t_ref[...], NN)
    absolute = both[:, :LANES] + both[:, LANES:]
    relative = [
        pltpu.roll(absolute[n : n + 8], (BAND // 2 - 4 * rows + 1 + n) % LANES, 1, stride=1, stride_axis=0)
        for n in range(0, 3 * rows, 8)
    ]
    relative = jnp.concatenate(relative, axis=0)
    share = rows // ncol
    out_ref[...] = jnp.zeros_like(out_ref)
    for g in range(3):
        row = wrap(lax.axis_index("row") + (g - 1), nrow)
        for c in range(ncol):
            at = (3 - g) * rows - (c + 1) * share
            out_ref[row * ncol + c] = relative[at : at + share]


def sum_kernel(ncol, nrow, got_ref, out_ref):
    total = None
    for step in (-1, 0, 1):
        row = wrap(lax.axis_index("row") + step, nrow)
        for c in range(ncol):
            part = got_ref[row * ncol + c]
            total = part if total is None else total + part
    for n in range(total.shape[0]):
        out_ref[n : n + 1, :] = total[total.shape[0] - 1 - n : total.shape[0] - n]


HBM = pl.BlockSpec(memory_space=pltpu.HBM)
SMEM = pl.BlockSpec(memory_space=pltpu.SMEM)
VMEM = pl.BlockSpec(memory_space=pltpu.VMEM)
VMEM_LIMIT = 20 * 1024 * 1024
PACK_LIMIT = 51 * 1024 * 1024
CHUNKS = 6


def on_device(weights, block_cols, counts, near_null, prior_ridge):
    rows, slots, size, _ = weights.shape
    total = block_cols.shape[1]
    nrow, ncol = lax.axis_size("row"), lax.axis_size("col")
    all_rows = rows * nrow
    f32, bf16 = jnp.float32, jnp.bfloat16
    array = jax.ShapeDtypeStruct
    scratch = pltpu.VMEM

    def call(kernel, out_shape, specs, scratches, *operands, limit=VMEM_LIMIT):
        return pl.pallas_call(
            kernel, out_shape=out_shape, in_specs=specs,
            out_specs=jax.tree.map(lambda _: VMEM, out_shape), scratch_shapes=scratches,
            compiler_params=pltpu.CompilerParams(vmem_limit_bytes=limit),
        )(*operands)

    def send(x, to):
        pairs = []
        for r in range(nrow):
            for c in range(ncol):
                nr, nc = to(r, c)
                pairs.append((r * ncol + c, (nr % nrow) * ncol + nc))
        return lax.ppermute(x, ("row", "col"), pairs)

    def partner(x):
        return send(x, lambda r, c: (r, c ^ 1))

    def across(x):
        return send(x, lambda r, c: (r, c ^ 2))

    def outward(x, d=0):
        return send(x, lambda r, c: (r + (1 if c % 2 == 0 else -1), c ^ d))

    cols = block_cols.T
    null_mine = outward(near_null)
    cols_mine = outward(cols)
    packed = call(
        pack_kernel, array((rows, size, 2 * slots * size), bf16), [HBM],
        [scratch(weights.shape, f32), pltpu.SemaphoreType.DMA((CHUNKS if rows % CHUNKS == 0 else 1,))],
        weights, limit=PACK_LIMIT)
    start = lax.axis_index("col") * slots
    targets = aim(all_rows, start, counts, lax.dynamic_slice_in_dim(cols, start, slots, 0))
    null_other = partner(null_mine)
    cols_other = partner(cols_mine)
    count = (slots // 2) * rows + -(-rows // 16) * 8
    block, unit = call(
        functools.partial(unit_kernel, size),
        [array((count, LANES), f32), array((3 * rows + 8, LANES), f32)],
        [SMEM] + [VMEM] * 5, [scratch((8 * rows + 8, size), f32), scratch((3 * rows + 8, LANES), f32)],
        targets, null_mine, null_other, near_null, prior_ridge, packed)
    hots = call(
        functools.partial(hot_kernel, slots, all_rows),
        [array((3 * rows + 1, total, LANES), bf16)] * 2 + [array((3 * rows, rows * total), bf16)],
        [VMEM] * 3,
        [scratch((3 * rows * total + total, LANES), f32)] * 2 + [scratch((rows * total + total, LANES), f32)],
        cols_mine, cols_other, cols)
    own = jnp.concatenate([block, partner(block)])
    diagonal = outward(own, 2)
    straight = outward(own)
    far = across(block)
    far_partner = partner(far)
    diagonal_partner = partner(diagonal)
    last = partner(straight)
    own_parts = call(
        functools.partial(own_kernel, size),
        [array((rows, total, LANES), bf16)] * 2
        + [array((rows, 2 * total, 2 * slots * size), bf16), array((rows, 2 * total, total), bf16)],
        [VMEM] * 5, [scratch((rows * total // 2 + total, LANES), f32)],
        own, far, far_partner, unit, packed)
    ready = call(
        functools.partial(ready_kernel, size, slots), [array((rows, total, LANES), bf16)] * 2,
        [VMEM] * 3, [scratch((rows * total // 2 + total, LANES), f32)],
        straight, diagonal, unit)
    parts = call(
        functools.partial(coarse_kernel, size, slots, ncol, nrow),
        array((nrow * ncol, rows // ncol, LANES), f32), [SMEM] + [VMEM] * 12,
        [
            scratch((rows * total // 2 + total, LANES), f32),
            scratch((3 * rows + 1, total, LANES), bf16),
            scratch((3 * rows + 1, total, LANES), bf16),
            scratch((rows, 2 * total, (slots + 1) * total), bf16),
            scratch((rows * total, 2 * LANES), bf16),
        ],
        targets, last, diagonal_partner, unit, *own_parts, *ready, *hots)
    got = lax.all_to_all(parts, ("row", "col"), 0, 0)
    return call(
        functools.partial(sum_kernel, ncol, nrow), array((rows // ncol, LANES), f32), [VMEM], [], got)


def solution(mesh):
    placed = (P("row", "col", None, None), P("row", None), P("row"), P("row", None), P("row", None))

    return jax.shard_map(on_device, mesh=mesh, in_specs=placed, out_specs=P(("row", "col"), None), check_vma=False)
```

```python
import functools

import jax
import jax.numpy as jnp
from jax import lax
from jax.experimental import pallas as pl
from jax.experimental.pallas import tpu as pltpu
from jax.sharding import PartitionSpec as P


H = 21
BAND = 128
LANES = 128

epsilon = 1e-06
relax_weight = 2.0 / 3.0

NT = (((1,), (1,)), ((), ()))
NN = (((1,), (0,)), ((), ()))


def mxu(a, b, dims):
    return lax.dot_general(a, b, dims, preferred_element_type=jnp.float32)


def split(x):
    hi = x.astype(jnp.bfloat16)
    lo = (x - hi.astype(jnp.float32)).astype(jnp.bfloat16)
    return hi, lo


def lane_iota(shape):
    return lax.broadcasted_iota(jnp.int32, shape, len(shape) - 1)


def row_iota(shape):
    return lax.broadcasted_iota(jnp.int32, shape, 0)


def wrap(x, count):
    x = jnp.where(x < 0, x + count, x)
    return jnp.where(x >= count, x - count, x)


def roll(x, by):
    return pltpu.roll(x, by % LANES, 1)


def pack_kernel(w_hbm, pack_ref, w_ref, sems):
    rows, slots, size, _ = w_ref.shape
    per = LANES // size
    chunks = sems.shape[0]
    step = rows // chunks
    copies = [
        pltpu.make_async_copy(w_hbm.at[pl.ds(n * step, step)], w_ref.at[pl.ds(n * step, step)], sems.at[n])
        for n in range(chunks)
    ]
    for copy in copies:
        copy.start()
    for i in range(rows):
        if i % step == 0:
            copies[i // step].wait()
        for p in range(slots // per):
            tile = jnp.concatenate([w_ref[i, per * p + h] for h in range(per)], axis=1)
            hi, lo = split(tile)
            pack_ref[i, :, 2 * p * LANES : (2 * p + 1) * LANES] = hi
            pack_ref[i, :, (2 * p + 1) * LANES : 2 * (p + 1) * LANES] = lo


def two_part(hi, lo):
    top = jnp.concatenate([hi, hi], axis=1)
    return jnp.concatenate([top, jnp.concatenate([lo, jnp.zeros_like(lo)], axis=1)], axis=0)


def aim(all_rows, start, counts, cols):
    slots, rows = cols.shape
    local = lane_iota((slots, rows))
    first = lax.axis_index("row") * rows
    at = wrap(cols - (first + local) + H, all_rows) + (rows - H) + local
    mirror = jnp.where(at < rows, at + 2 * rows, jnp.where(at >= 2 * rows, at - 2 * rows, at))
    at = jnp.where(lax.axis_index("col") % 2 == 0, at, mirror)
    return jnp.where(row_iota((slots, rows)) + start < counts[None, :], at, 3 * rows)


def unit_kernel(size, targets, mine_ref, other_ref, own_ref, ridge_ref, pack_ref,
                block_ref, unit_ref, acc_ref, one_ref):
    rows = own_ref.shape[0]
    slots = pack_ref.shape[2] // (2 * size)
    column = lax.axis_index("col")
    for g, ref in enumerate((mine_ref, own_ref, other_ref)):
        x = ref[...]
        unit = x / jnp.sqrt(jnp.sum(x * x, axis=1, keepdims=True) + epsilon)
        unit_ref[g * rows : (g + 1) * rows, :] = jnp.concatenate([unit, unit], axis=1)
    unit_ref[3 * rows :, :] = jnp.zeros((8, LANES), jnp.float32)
    one_ref[: 3 * rows, :] = jnp.ones((3 * rows, LANES), jnp.float32)
    one_ref[3 * rows :, :] = jnp.zeros((8, LANES), jnp.float32)
    row8 = row_iota((8, LANES))
    half = lane_iota((8, LANES)) // size
    for i in range(rows):
        both = None
        for p in range(slots // 2):
            tile = jnp.zeros((8, LANES), jnp.float32)
            for h in range(2):
                k = 2 * p + h
                t = targets[k, i]
                vec = jnp.broadcast_to(unit_ref[pl.ds(t, 1), :], (8, LANES))
                one = jnp.broadcast_to(one_ref[pl.ds(t, 1), :], (8, LANES))
                tile = jnp.where((row8 == k) & (half == h), vec, tile)
                tile = jnp.where((row8 == slots) & (half == h), one, tile)
            term = mxu(two_part(*split(tile)), pack_ref[i, :, 2 * p * LANES : 2 * (p + 1) * LANES], NT)
            both = term if both is None else both + term
        acc_ref[8 * i : 8 * i + 8, :] = both[:8] + both[8:]
    plane = [acc_ref[pl.ds(k, rows, stride=8), :] for k in range(slots + 1)]
    for p in range(slots // 2):
        block_ref[p * rows : (p + 1) * rows, :] = jnp.concatenate(plane[2 * p : 2 * p + 2], axis=1)
    degree = plane[slots] + jnp.where(column == 0, ridge_ref[...], 0.0)
    keep = block_ref.shape[0] - (slots // 2) * rows
    rest = jnp.concatenate([degree[keep:], jnp.zeros((2 * keep - rows, size), jnp.float32)], axis=0)
    block_ref[(slots // 2) * rows :, :] = jnp.concatenate([degree[:keep], rest], axis=1)


def hot_kernel(slots, all_rows, mine_ref, other_ref, own_ref, even_ref, odd_ref, turned_ref,
               even_tmp, odd_tmp, turn_tmp):
    total, rows = own_ref.shape
    column = lax.axis_index("col")
    reach = jnp.where(column % 2 == 0, rows, -rows)
    lane = lane_iota((rows, LANES))
    pairs = total // 2
    for g, ref in enumerate((mine_ref, own_ref, other_ref)):
        cols = ref[...]
        local = row_iota((rows, LANES)) + (g - 1) * reach
        cols = jnp.concatenate([cols, jnp.zeros((total, LANES - rows), jnp.int32)], axis=1)
        cols = jnp.concatenate([cols, jnp.zeros((LANES - total, LANES), jnp.int32)], axis=0)
        cols = cols.T[:rows]
        base = lax.axis_index("row") * rows + local
        where = wrap(wrap(cols - base + H, all_rows), all_rows) - H + local + 2 * rows
        bit = slots
        while bit < total:
            swapped = jnp.where((lane // bit) % 2 == 1, roll(where, bit), roll(where, -bit))
            where = jnp.where((column * slots // bit) % 2 == 1, swapped, where)
            bit *= 2
        for s in range(total):
            spread = jnp.broadcast_to(where[:, s : s + 1], (rows, LANES))
            hot = jnp.where(spread == lane, 1.0, 0.0)
            at, other = s // 2 + (s % 2) * pairs, s // 2 + (1 - s % 2) * pairs
            even_tmp[pl.ds(g * rows * total + at, rows, stride=total), :] = hot
            odd_tmp[pl.ds(g * rows * total + other, rows, stride=total), :] = hot
            if g == 1:
                turn_tmp[pl.ds(at, rows, stride=total), :] = jnp.where(
                    spread == LANES - 1 - lane, 1.0, 0.0)
    for j in range(3 * rows):
        even_ref[j] = even_tmp[j * total : (j + 1) * total, :].astype(jnp.bfloat16)
        odd_ref[j] = odd_tmp[j * total : (j + 1) * total, :].astype(jnp.bfloat16)
    even_ref[3 * rows] = jnp.zeros((total, LANES), jnp.bfloat16)
    odd_ref[3 * rows] = jnp.zeros((total, LANES), jnp.bfloat16)
    for n in range(rows * total // LANES):
        lanes = slice(n * LANES, (n + 1) * LANES)
        turned = turn_tmp[lanes, :].T
        turned_ref[:, lanes] = turned[LANES - 4 * rows : LANES - rows].astype(jnp.bfloat16)


def prolong_rows(planes, unit, column, slots, size, p_ref, first, store):
    rows, ncol = unit.shape[0], len(planes)
    pairs = slots // 2
    half = pairs * ncol
    low_half = lane_iota((rows, LANES)) < size
    degree = sum(block(pairs * rows, None) for block in planes)
    keep = degree.shape[0]
    degree = jnp.concatenate([degree, roll(degree, size)[: rows - keep]], axis=0)
    inverse = relax_weight / jnp.where(low_half, degree, 1.0)
    inverse = jnp.where(low_half, inverse, roll(inverse, size))
    own_term = jnp.where(low_half, (1.0 - relax_weight) * unit, 0.0)
    for d in range(ncol):
        for p in range(pairs):
            v = planes[d](p * rows, (p + 1) * rows) * inverse
            if p == 0:
                v = v + jnp.where(column == d, own_term, 0.0)
            p_ref[pl.ds(first * half + d * pairs + p, rows, stride=half), :] = v
    for j in range(first, first + rows):
        v = p_ref[j * half : (j + 1) * half, :]
        store(j, jnp.concatenate([v, roll(v, size)], axis=0))


def block_of(ref, index, size):
    def rows_of(start, stop):
        return ref[index * size + start : index * size + (size if stop is None else stop), :]

    return rows_of


def own_kernel(size, own_ref, far_ref, far_partner_ref, unit_ref, pack_ref,
               qh_ref, ql_ref, v_ref, diagonal_ref, p_ref):
    rows, total, _ = qh_ref.shape
    slots = pack_ref.shape[2] // (2 * size)
    count = far_ref.shape[0]
    degree = own_ref[(slots // 2) * rows : count, :]
    degree = jnp.concatenate([degree, roll(degree, size)[: rows - degree.shape[0]]], axis=0)
    low_half = lane_iota((total, LANES)) < size
    kept = []

    def store(i, q):
        hi, lo = split(q)
        qh_ref[i], ql_ref[i] = hi, lo
        term = q[:, :size] * degree[i : i + 1, :size]
        kept.append((jnp.concatenate([hi[:, :size], lo[:, :size]], axis=0),
                     jnp.where(low_half, q, roll(q, size)), jnp.concatenate(split(term), axis=1)))

    group = [(own_ref, 0), (own_ref, 1), (far_ref, 0), (far_partner_ref, 0)]
    blocks = [block_of(ref, index, count) for ref, index in group]
    prolong_rows(blocks, unit_ref[rows : 2 * rows, :], lax.axis_index("col"), slots, size, p_ref, 0, store)
    for i, (left, _, _) in enumerate(kept):
        both = mxu(left, pack_ref[i], NN)
        for p in range(slots // 2):
            at = 2 * p * LANES
            hi_lanes, lo_lanes = slice(at, at + LANES), slice(at + LANES, at + 2 * LANES)
            v = both[:total, hi_lanes] + both[:total, lo_lanes] + both[total:, hi_lanes]
            v_ref[i, :, at : at + 2 * LANES] = two_part(*split(-v))
    for i, (_, doubled, term) in enumerate(kept):
        hi, lo = split(doubled)
        both = mxu(jnp.concatenate([hi, jnp.where(low_half, lo, jnp.zeros_like(lo))], axis=0), term, NT)
        diagonal_ref[i] = jnp.concatenate(split(both[:total] + both[total:]), axis=0)


def ready_kernel(size, slots, straight_ref, diagonal_ref, unit_ref, qh_ref, ql_ref, p_ref):
    rows = qh_ref.shape[0]
    count = straight_ref.shape[0] // 2

    def store(j, q):
        qh_ref[j], ql_ref[j] = split(q)

    blocks = [block_of(ref, index, count) for ref in (straight_ref, diagonal_ref) for index in range(2)]
    prolong_rows(blocks, unit_ref[:rows, :], lax.axis_index("col"), slots, size, p_ref, 0, store)


def coarse_kernel(size, slots, ncol, nrow, targets, last_ref, diagonal_partner_ref, unit_ref, own_h_ref, own_l_ref, v_ref,
                  diagonal_ref, mine_h_ref, mine_l_ref, even_ref, odd_ref, turned_ref, out_ref,
                  p_ref, qh_ref, ql_ref, s_ref, t_ref):
    rows, total, _ = own_h_ref.shape
    pairs = slots // 2
    column = lax.axis_index("col")
    count = last_ref.shape[0] // 2

    def store(j, q):
        qh_ref[2 * rows + j], ql_ref[2 * rows + j] = split(q)

    blocks = [
        block_of(ref, index, count) for ref in (last_ref, diagonal_partner_ref) for index in (1, 0)
    ]
    prolong_rows(blocks, unit_ref[2 * rows : 3 * rows, :], column, slots, size, p_ref, 0, store)
    for table, mine, own in ((qh_ref, mine_h_ref, own_h_ref), (ql_ref, mine_l_ref, own_l_ref)):
        table[:rows] = mine[...]
        table[rows : 2 * rows] = own[...]
        table[3 * rows] = jnp.zeros((total, LANES), jnp.bfloat16)
    tile_half = lane_iota((total, LANES)) // size
    zero = jnp.zeros((total, LANES), jnp.bfloat16)
    tiles = [[targets[k, i] for k in range(slots)] for i in range(rows)]
    for i in range(rows):
        for p in range(pairs):
            right = []
            for h in range(2):
                t = tiles[i][2 * p + h]
                parts = [jnp.where(tile_half == h, table[t], zero) for table in (qh_ref, ql_ref)]
                right.append(jnp.concatenate(parts, axis=1))
            both = mxu(v_ref[i, :, 2 * p * LANES : 2 * (p + 1) * LANES], jnp.concatenate(right, axis=0), NT)
            at = slice(2 * p * total, 2 * (p + 1) * total)
            s_ref[i, :total, at], s_ref[i, total:, at] = split(both[:total] + both[total:])
        s_ref[i, :, slots * total :] = diagonal_ref[i]
    for i in range(rows):
        hot = [(even_ref if k % 2 == 0 else odd_ref)[tiles[i][k]] for k in range(slots)]
        both = mxu(s_ref[i], jnp.concatenate(hot + [even_ref[rows + i]], axis=0), NN)
        at = slice(i * total, (i + 1) * total)
        t_ref[at, :LANES], t_ref[at, LANES:] = split(both[:total] + both[total:])
    both = mxu(turned_ref[...], t_ref[...], NN)
    absolute = both[:, :LANES] + both[:, LANES:]
    relative = [
        pltpu.roll(absolute[n : n + 8], (BAND // 2 - 4 * rows + 1 + n) % LANES, 1, stride=1, stride_axis=0)
        for n in range(0, 3 * rows, 8)
    ]
    relative = jnp.concatenate(relative, axis=0)
    share = rows // ncol
    out_ref[...] = jnp.zeros_like(out_ref)
    for g in range(3):
        row = wrap(lax.axis_index("row") + (g - 1), nrow)
        for c in range(ncol):
            at = (3 - g) * rows - (c + 1) * share
            for n in range(share // 2):
                out_ref[(row * ncol + c) * (share // 2) + n] = relative[at + 2 * n : at + 2 * n + 2]


def sum_kernel(ncol, nrow, got_ref, out_ref):
    share = out_ref.shape[0]
    for n in range(share // 2):
        total = None
        for step in (-1, 0, 1):
            row = wrap(lax.axis_index("row") + step, nrow)
            for c in range(ncol):
                part = got_ref[(row * ncol + c) * (share // 2) + n]
                total = part if total is None else total + part
        for m in range(2):
            at = share - 1 - 2 * n - m
            out_ref[at : at + 1, :] = total[m : m + 1]


HBM = pl.BlockSpec(memory_space=pltpu.HBM)
SMEM = pl.BlockSpec(memory_space=pltpu.SMEM)
VMEM = pl.BlockSpec(memory_space=pltpu.VMEM)
VMEM_LIMIT = 20 * 1024 * 1024
PACK_LIMIT = 51 * 1024 * 1024
CHUNKS = 6


def on_device(weights, block_cols, counts, near_null, prior_ridge):
    rows, slots, size, _ = weights.shape
    total = block_cols.shape[1]
    nrow, ncol = lax.axis_size("row"), lax.axis_size("col")
    all_rows = rows * nrow
    f32, bf16 = jnp.float32, jnp.bfloat16
    array = jax.ShapeDtypeStruct
    scratch = pltpu.VMEM

    def call(kernel, out_shape, specs, scratches, *operands, limit=VMEM_LIMIT):
        return pl.pallas_call(
            kernel, out_shape=out_shape, in_specs=specs,
            out_specs=jax.tree.map(lambda _: VMEM, out_shape), scratch_shapes=scratches,
            compiler_params=pltpu.CompilerParams(vmem_limit_bytes=limit),
        )(*operands)

    def send(x, to):
        pairs = []
        for r in range(nrow):
            for c in range(ncol):
                nr, nc = to(r, c)
                pairs.append((r * ncol + c, (nr % nrow) * ncol + nc))
        return lax.ppermute(x, ("row", "col"), pairs)

    def partner(x):
        return send(x, lambda r, c: (r, c ^ 1))

    def across(x):
        return send(x, lambda r, c: (r, c ^ 2))

    def outward(x, d=0):
        return send(x, lambda r, c: (r + (1 if c % 2 == 0 else -1), c ^ d))

    cols = block_cols.T
    null_mine = outward(near_null)
    cols_mine = outward(cols)
    packed = call(
        pack_kernel, array((rows, size, 2 * slots * size), bf16), [HBM],
        [scratch(weights.shape, f32), pltpu.SemaphoreType.DMA((CHUNKS if rows % CHUNKS == 0 else 1,))],
        weights, limit=PACK_LIMIT)
    start = lax.axis_index("col") * slots
    targets = aim(all_rows, start, counts, lax.dynamic_slice_in_dim(cols, start, slots, 0))
    null_other = partner(null_mine)
    cols_other = partner(cols_mine)
    count = (slots // 2) * rows + -(-rows // 16) * 8
    block, unit = call(
        functools.partial(unit_kernel, size),
        [array((count, LANES), f32), array((3 * rows + 8, LANES), f32)],
        [SMEM] + [VMEM] * 5, [scratch((8 * rows + 8, size), f32), scratch((3 * rows + 8, LANES), f32)],
        targets, null_mine, null_other, near_null, prior_ridge, packed)
    hots = call(
        functools.partial(hot_kernel, slots, all_rows),
        [array((3 * rows + 1, total, LANES), bf16)] * 2 + [array((3 * rows, rows * total), bf16)],
        [VMEM] * 3,
        [scratch((3 * rows * total + total, LANES), f32)] * 2 + [scratch((rows * total + total, LANES), f32)],
        cols_mine, cols_other, cols)
    own = jnp.concatenate([block, partner(block)])
    diagonal = outward(own, 2)
    straight = outward(own)
    far = across(block)
    far_partner = partner(far)
    diagonal_partner = partner(diagonal)
    last = partner(straight)
    own_parts = call(
        functools.partial(own_kernel, size),
        [array((rows, total, LANES), bf16)] * 2
        + [array((rows, 2 * total, 2 * slots * size), bf16), array((rows, 2 * total, total), bf16)],
        [VMEM] * 5, [scratch((rows * total // 2 + total, LANES), f32)],
        own, far, far_partner, unit, packed)
    ready = call(
        functools.partial(ready_kernel, size, slots), [array((rows, total, LANES), bf16)] * 2,
        [VMEM] * 3, [scratch((rows * total // 2 + total, LANES), f32)],
        straight, diagonal, unit)
    parts = call(
        functools.partial(coarse_kernel, size, slots, ncol, nrow),
        array((nrow * rows // 2, 2, LANES), f32), [SMEM] + [VMEM] * 12,
        [
            scratch((rows * total // 2 + total, LANES), f32),
            scratch((3 * rows + 1, total, LANES), bf16),
            scratch((3 * rows + 1, total, LANES), bf16),
            scratch((rows, 2 * total, (slots + 1) * total), bf16),
            scratch((rows * total, 2 * LANES), bf16),
        ],
        targets, last, diagonal_partner, unit, *own_parts, *ready, *hots)
    got = lax.all_to_all(parts, ("row", "col"), 0, 0, tiled=True)
    return call(
        functools.partial(sum_kernel, ncol, nrow), array((rows // ncol, LANES), f32), [VMEM], [], got)


def solution(mesh):
    placed = (P("row", "col", None, None), P("row", None), P("row"), P("row", None), P("row", None))

    return jax.shard_map(on_device, mesh=mesh, in_specs=placed, out_specs=P(("row", "col"), None), check_vma=False)
```

```python
import functools

import jax
import jax.numpy as jnp
from jax import lax
from jax.experimental import pallas as pl
from jax.experimental.pallas import tpu as pltpu
from jax.sharding import PartitionSpec as P


H = 21
BAND = 128
LANES = 128

epsilon = 1e-06
relax_weight = 2.0 / 3.0

NT = (((1,), (1,)), ((), ()))
NN = (((1,), (0,)), ((), ()))


def mxu(a, b, dims):
    return lax.dot_general(a, b, dims, preferred_element_type=jnp.float32)


def split(x):
    hi = x.astype(jnp.bfloat16)
    lo = (x - hi.astype(jnp.float32)).astype(jnp.bfloat16)
    return hi, lo


def lane_iota(shape):
    return lax.broadcasted_iota(jnp.int32, shape, len(shape) - 1)


def row_iota(shape):
    return lax.broadcasted_iota(jnp.int32, shape, 0)


def wrap(x, count):
    x = jnp.where(x < 0, x + count, x)
    return jnp.where(x >= count, x - count, x)


def roll(x, by):
    return pltpu.roll(x, by % LANES, 1)


def pack_kernel(w_hbm, pack_ref, w_ref, sems):
    rows, slots, size, _ = w_ref.shape
    per = LANES // size
    chunks = sems.shape[0]
    step = rows // chunks
    copies = [
        pltpu.make_async_copy(w_hbm.at[pl.ds(n * step, step)], w_ref.at[pl.ds(n * step, step)], sems.at[n])
        for n in range(chunks)
    ]
    for copy in copies:
        copy.start()
    for i in range(rows):
        if i % step == 0:
            copies[i // step].wait()
        for p in range(slots // per):
            tile = jnp.concatenate([w_ref[i, per * p + h] for h in range(per)], axis=1)
            hi, lo = split(tile)
            pack_ref[i, :, 2 * p * LANES : (2 * p + 1) * LANES] = hi
            pack_ref[i, :, (2 * p + 1) * LANES : 2 * (p + 1) * LANES] = lo


def two_part(hi, lo):
    top = jnp.concatenate([hi, hi], axis=1)
    return jnp.concatenate([top, jnp.concatenate([lo, jnp.zeros_like(lo)], axis=1)], axis=0)


def aim(all_rows, start, counts, cols):
    slots, rows = cols.shape
    local = lane_iota((slots, rows))
    first = lax.axis_index("row") * rows
    at = wrap(cols - (first + local) + H, all_rows) + (rows - H) + local
    mirror = jnp.where(at < rows, at + 2 * rows, jnp.where(at >= 2 * rows, at - 2 * rows, at))
    at = jnp.where(lax.axis_index("col") % 2 == 0, at, mirror)
    return jnp.where(row_iota((slots, rows)) + start < counts[None, :], at, 3 * rows)


def unit_kernel(size, targets, mine_ref, other_ref, own_ref, ridge_ref, pack_ref,
                block_ref, unit_ref, acc_ref, one_ref):
    rows = own_ref.shape[0]
    slots = pack_ref.shape[2] // (2 * size)
    column = lax.axis_index("col")
    for g, ref in enumerate((mine_ref, own_ref, other_ref)):
        x = ref[...]
        unit = x / jnp.sqrt(jnp.sum(x * x, axis=1, keepdims=True) + epsilon)
        unit_ref[g * rows : (g + 1) * rows, :] = jnp.concatenate([unit, unit], axis=1)
    unit_ref[3 * rows :, :] = jnp.zeros((8, LANES), jnp.float32)
    one_ref[: 3 * rows, :] = jnp.ones((3 * rows, LANES), jnp.float32)
    one_ref[3 * rows :, :] = jnp.zeros((8, LANES), jnp.float32)
    row8 = row_iota((8, LANES))
    half = lane_iota((8, LANES)) // size
    for i in range(rows):
        both = None
        for p in range(slots // 2):
            tile = jnp.zeros((8, LANES), jnp.float32)
            for h in range(2):
                k = 2 * p + h
                t = targets[k, i]
                vec = jnp.broadcast_to(unit_ref[pl.ds(t, 1), :], (8, LANES))
                one = jnp.broadcast_to(one_ref[pl.ds(t, 1), :], (8, LANES))
                tile = jnp.where((row8 == k) & (half == h), vec, tile)
                tile = jnp.where((row8 == slots) & (half == h), one, tile)
            term = mxu(two_part(*split(tile)), pack_ref[i, :, 2 * p * LANES : 2 * (p + 1) * LANES], NT)
            both = term if both is None else both + term
        acc_ref[8 * i : 8 * i + 8, :] = both[:8] + both[8:]
    plane = [acc_ref[pl.ds(k, rows, stride=8), :] for k in range(slots + 1)]
    for p in range(slots // 2):
        block_ref[p * rows : (p + 1) * rows, :] = jnp.concatenate(plane[2 * p : 2 * p + 2], axis=1)
    degree = plane[slots] + jnp.where(column == 0, ridge_ref[...], 0.0)
    keep = block_ref.shape[0] - (slots // 2) * rows
    rest = jnp.concatenate([degree[keep:], jnp.zeros((2 * keep - rows, size), jnp.float32)], axis=0)
    block_ref[(slots // 2) * rows :, :] = jnp.concatenate([degree[:keep], rest], axis=1)


def hot_kernel(slots, all_rows, mine_ref, other_ref, own_ref, even_ref, odd_ref, turned_ref,
               even_tmp, odd_tmp, turn_tmp):
    total, rows = own_ref.shape
    column = lax.axis_index("col")
    reach = jnp.where(column % 2 == 0, rows, -rows)
    lane = lane_iota((rows, LANES))
    pairs = total // 2
    for g, ref in enumerate((mine_ref, own_ref, other_ref)):
        cols = ref[...]
        local = row_iota((rows, LANES)) + (g - 1) * reach
        cols = jnp.concatenate([cols, jnp.zeros((total, LANES - rows), jnp.int32)], axis=1)
        cols = jnp.concatenate([cols, jnp.zeros((LANES - total, LANES), jnp.int32)], axis=0)
        cols = cols.T[:rows]
        base = lax.axis_index("row") * rows + local
        where = wrap(wrap(cols - base + H, all_rows), all_rows) - H + local + 2 * rows
        bit = slots
        while bit < total:
            swapped = jnp.where((lane // bit) % 2 == 1, roll(where, bit), roll(where, -bit))
            where = jnp.where((column * slots // bit) % 2 == 1, swapped, where)
            bit *= 2
        for s in range(total):
            spread = jnp.broadcast_to(where[:, s : s + 1], (rows, LANES))
            hot = jnp.where(spread == lane, 1.0, 0.0)
            at, other = s // 2 + (s % 2) * pairs, s // 2 + (1 - s % 2) * pairs
            even_tmp[pl.ds(g * rows * total + at, rows, stride=total), :] = hot
            odd_tmp[pl.ds(g * rows * total + other, rows, stride=total), :] = hot
            if g == 1:
                turn_tmp[pl.ds(at, rows, stride=total), :] = jnp.where(
                    spread == LANES - 1 - lane, 1.0, 0.0)
    for j in range(3 * rows):
        even_ref[j] = even_tmp[j * total : (j + 1) * total, :].astype(jnp.bfloat16)
        odd_ref[j] = odd_tmp[j * total : (j + 1) * total, :].astype(jnp.bfloat16)
    even_ref[3 * rows] = jnp.zeros((total, LANES), jnp.bfloat16)
    odd_ref[3 * rows] = jnp.zeros((total, LANES), jnp.bfloat16)
    for n in range(rows * total // LANES):
        lanes = slice(n * LANES, (n + 1) * LANES)
        turned = turn_tmp[lanes, :].T
        turned_ref[:, lanes] = turned[LANES - 4 * rows : LANES - rows].astype(jnp.bfloat16)


def prolong_rows(planes, unit, column, slots, size, p_ref, first, store):
    rows, ncol = unit.shape[0], len(planes)
    pairs = slots // 2
    half = pairs * ncol
    low_half = lane_iota((rows, LANES)) < size
    degree = sum(block(pairs * rows, None) for block in planes)
    keep = degree.shape[0]
    degree = jnp.concatenate([degree, roll(degree, size)[: rows - keep]], axis=0)
    inverse = relax_weight / jnp.where(low_half, degree, 1.0)
    inverse = jnp.where(low_half, inverse, roll(inverse, size))
    own_term = jnp.where(low_half, (1.0 - relax_weight) * unit, 0.0)
    for d in range(ncol):
        for p in range(pairs):
            v = planes[d](p * rows, (p + 1) * rows) * inverse
            if p == 0:
                v = v + jnp.where(column == d, own_term, 0.0)
            p_ref[pl.ds(first * half + d * pairs + p, rows, stride=half), :] = v
    for j in range(first, first + rows):
        v = p_ref[j * half : (j + 1) * half, :]
        store(j, jnp.concatenate([v, roll(v, size)], axis=0))


def block_of(ref, index, size):
    def rows_of(start, stop):
        return ref[index * size + start : index * size + (size if stop is None else stop), :]

    return rows_of


def own_kernel(size, own_ref, far_ref, far_partner_ref, unit_ref, pack_ref,
               qh_ref, ql_ref, v_ref, diagonal_ref, p_ref):
    rows, total, _ = qh_ref.shape
    slots = pack_ref.shape[2] // (2 * size)
    count = far_ref.shape[0]
    degree = own_ref[(slots // 2) * rows : count, :]
    degree = jnp.concatenate([degree, roll(degree, size)[: rows - degree.shape[0]]], axis=0)
    low_half = lane_iota((total, LANES)) < size
    kept = []

    def store(i, q):
        hi, lo = split(q)
        qh_ref[i], ql_ref[i] = hi, lo
        term = q[:, :size] * degree[i : i + 1, :size]
        kept.append((jnp.concatenate([hi[:, :size], lo[:, :size]], axis=0),
                     jnp.where(low_half, q, roll(q, size)), jnp.concatenate(split(term), axis=1)))

    group = [(own_ref, 0), (own_ref, 1), (far_ref, 0), (far_partner_ref, 0)]
    blocks = [block_of(ref, index, count) for ref, index in group]
    prolong_rows(blocks, unit_ref[rows : 2 * rows, :], lax.axis_index("col"), slots, size, p_ref, 0, store)
    for i, (left, _, _) in enumerate(kept):
        both = mxu(left, pack_ref[i], NN)
        for p in range(slots // 2):
            at = 2 * p * LANES
            hi_lanes, lo_lanes = slice(at, at + LANES), slice(at + LANES, at + 2 * LANES)
            v = both[:total, hi_lanes] + both[:total, lo_lanes] + both[total:, hi_lanes]
            v_ref[i, :, at : at + 2 * LANES] = two_part(*split(-v))
    for i, (_, doubled, term) in enumerate(kept):
        hi, lo = split(doubled)
        both = mxu(jnp.concatenate([hi, jnp.where(low_half, lo, jnp.zeros_like(lo))], axis=0), term, NT)
        diagonal_ref[i] = jnp.concatenate(split(both[:total] + both[total:]), axis=0)


def ready_kernel(size, slots, straight_ref, diagonal_ref, unit_ref, qh_ref, ql_ref, p_ref):
    rows = qh_ref.shape[0]
    count = straight_ref.shape[0] // 2

    def store(j, q):
        qh_ref[j], ql_ref[j] = split(q)

    blocks = [block_of(ref, index, count) for ref in (straight_ref, diagonal_ref) for index in range(2)]
    prolong_rows(blocks, unit_ref[:rows, :], lax.axis_index("col"), slots, size, p_ref, 0, store)


def rows_kernel(size, slots, straight_ref, diagonal_ref, own_ref, far_ref, far_partner_ref, unit_ref, pack_ref,
                qh_ref, ql_ref, v_ref, term_ref, mine_h_ref, mine_l_ref, p_ref, mine_p_ref):
    ready_kernel(size, slots, straight_ref, diagonal_ref, unit_ref, mine_h_ref, mine_l_ref, mine_p_ref)
    own_kernel(size, own_ref, far_ref, far_partner_ref, unit_ref, pack_ref,
               qh_ref, ql_ref, v_ref, term_ref, p_ref)


def coarse_kernel(size, slots, ncol, nrow, targets, last_ref, diagonal_partner_ref, unit_ref, own_h_ref, own_l_ref, v_ref,
                  diagonal_ref, mine_h_ref, mine_l_ref, even_ref, odd_ref, turned_ref, out_ref,
                  p_ref, qh_ref, ql_ref, s_ref, t_ref):
    rows, total, _ = own_h_ref.shape
    pairs = slots // 2
    column = lax.axis_index("col")
    count = last_ref.shape[0] // 2

    def store(j, q):
        qh_ref[2 * rows + j], ql_ref[2 * rows + j] = split(q)

    blocks = [
        block_of(ref, index, count) for ref in (last_ref, diagonal_partner_ref) for index in (1, 0)
    ]
    prolong_rows(blocks, unit_ref[2 * rows : 3 * rows, :], column, slots, size, p_ref, 0, store)
    for table, mine, own in ((qh_ref, mine_h_ref, own_h_ref), (ql_ref, mine_l_ref, own_l_ref)):
        table[:rows] = mine[...]
        table[rows : 2 * rows] = own[...]
        table[3 * rows] = jnp.zeros((total, LANES), jnp.bfloat16)
    tile_half = lane_iota((total, LANES)) // size
    zero = jnp.zeros((total, LANES), jnp.bfloat16)
    tiles = [[targets[k, i] for k in range(slots)] for i in range(rows)]
    for i in range(rows):
        for p in range(pairs):
            right = []
            for h in range(2):
                t = tiles[i][2 * p + h]
                parts = [jnp.where(tile_half == h, table[t], zero) for table in (qh_ref, ql_ref)]
                right.append(jnp.concatenate(parts, axis=1))
            both = mxu(v_ref[i, :, 2 * p * LANES : 2 * (p + 1) * LANES], jnp.concatenate(right, axis=0), NT)
            at = slice(2 * p * total, 2 * (p + 1) * total)
            s_ref[i, :total, at], s_ref[i, total:, at] = split(both[:total] + both[total:])
        s_ref[i, :, slots * total :] = diagonal_ref[i]
    for i in range(rows):
        hot = [(even_ref if k % 2 == 0 else odd_ref)[tiles[i][k]] for k in range(slots)]
        both = mxu(s_ref[i], jnp.concatenate(hot + [even_ref[rows + i]], axis=0), NN)
        at = slice(i * total, (i + 1) * total)
        t_ref[at, :LANES], t_ref[at, LANES:] = split(both[:total] + both[total:])
    both = mxu(turned_ref[...], t_ref[...], NN)
    absolute = both[:, :LANES] + both[:, LANES:]
    relative = [
        pltpu.roll(absolute[n : n + 8], (BAND // 2 - 4 * rows + 1 + n) % LANES, 1, stride=1, stride_axis=0)
        for n in range(0, 3 * rows, 8)
    ]
    relative = jnp.concatenate(relative, axis=0)
    share = rows // ncol
    out_ref[...] = jnp.zeros_like(out_ref)
    for g in range(3):
        row = wrap(lax.axis_index("row") + (g - 1), nrow)
        for c in range(ncol):
            at = (3 - g) * rows - (c + 1) * share
            for n in range(share // 2):
                out_ref[(row * ncol + c) * (share // 2) + n] = relative[at + 2 * n : at + 2 * n + 2]


def sum_kernel(ncol, nrow, got_ref, out_ref):
    share = out_ref.shape[0]
    for n in range(share // 2):
        total = None
        for step in (-1, 0, 1):
            row = wrap(lax.axis_index("row") + step, nrow)
            for c in range(ncol):
                part = got_ref[(row * ncol + c) * (share // 2) + n]
                total = part if total is None else total + part
        for m in range(2):
            at = share - 1 - 2 * n - m
            out_ref[at : at + 1, :] = total[m : m + 1]


HBM = pl.BlockSpec(memory_space=pltpu.HBM)
SMEM = pl.BlockSpec(memory_space=pltpu.SMEM)
VMEM = pl.BlockSpec(memory_space=pltpu.VMEM)
VMEM_LIMIT = 20 * 1024 * 1024
PACK_LIMIT = 51 * 1024 * 1024
CHUNKS = 6


def on_device(weights, block_cols, counts, near_null, prior_ridge):
    rows, slots, size, _ = weights.shape
    total = block_cols.shape[1]
    nrow, ncol = lax.axis_size("row"), lax.axis_size("col")
    all_rows = rows * nrow
    f32, bf16 = jnp.float32, jnp.bfloat16
    array = jax.ShapeDtypeStruct
    scratch = pltpu.VMEM

    def call(kernel, out_shape, specs, scratches, *operands, limit=VMEM_LIMIT):
        return pl.pallas_call(
            kernel, out_shape=out_shape, in_specs=specs,
            out_specs=jax.tree.map(lambda _: VMEM, out_shape), scratch_shapes=scratches,
            compiler_params=pltpu.CompilerParams(vmem_limit_bytes=limit),
        )(*operands)

    def send(x, to):
        pairs = []
        for r in range(nrow):
            for c in range(ncol):
                nr, nc = to(r, c)
                pairs.append((r * ncol + c, (nr % nrow) * ncol + nc))
        return lax.ppermute(x, ("row", "col"), pairs)

    def partner(x):
        return send(x, lambda r, c: (r, c ^ 1))

    def across(x):
        return send(x, lambda r, c: (r, c ^ 2))

    def outward(x, d=0):
        return send(x, lambda r, c: (r + (1 if c % 2 == 0 else -1), c ^ d))

    cols = block_cols.T
    null_mine = outward(near_null)
    cols_mine = outward(cols)
    packed = call(
        pack_kernel, array((rows, size, 2 * slots * size), bf16), [HBM],
        [scratch(weights.shape, f32), pltpu.SemaphoreType.DMA((CHUNKS if rows % CHUNKS == 0 else 1,))],
        weights, limit=PACK_LIMIT)
    start = lax.axis_index("col") * slots
    targets = aim(all_rows, start, counts, lax.dynamic_slice_in_dim(cols, start, slots, 0))
    null_other = partner(null_mine)
    cols_other = partner(cols_mine)
    count = (slots // 2) * rows + -(-rows // 16) * 8
    block, unit = call(
        functools.partial(unit_kernel, size),
        [array((count, LANES), f32), array((3 * rows + 8, LANES), f32)],
        [SMEM] + [VMEM] * 5, [scratch((8 * rows + 8, size), f32), scratch((3 * rows + 8, LANES), f32)],
        targets, null_mine, null_other, near_null, prior_ridge, packed)
    hots = call(
        functools.partial(hot_kernel, slots, all_rows),
        [array((3 * rows + 1, total, LANES), bf16)] * 2 + [array((3 * rows, rows * total), bf16)],
        [VMEM] * 3,
        [scratch((3 * rows * total + total, LANES), f32)] * 2 + [scratch((rows * total + total, LANES), f32)],
        cols_mine, cols_other, cols)
    own = jnp.concatenate([block, partner(block)])
    diagonal = outward(own, 2)
    straight = outward(own)
    far = across(block)
    far_partner = partner(far)
    diagonal_partner = partner(diagonal)
    last = partner(straight)
    made = call(
        functools.partial(rows_kernel, size, slots),
        [array((rows, total, LANES), bf16)] * 2
        + [array((rows, 2 * total, 2 * slots * size), bf16), array((rows, 2 * total, total), bf16)]
        + [array((rows, total, LANES), bf16)] * 2,
        [VMEM] * 7, [scratch((rows * total // 2 + total, LANES), f32)] * 2,
        straight, diagonal, own, far, far_partner, unit, packed)
    parts = call(
        functools.partial(coarse_kernel, size, slots, ncol, nrow),
        array((nrow * rows // 2, 2, LANES), f32), [SMEM] + [VMEM] * 12,
        [
            scratch((rows * total // 2 + total, LANES), f32),
            scratch((3 * rows + 1, total, LANES), bf16),
            scratch((3 * rows + 1, total, LANES), bf16),
            scratch((rows, 2 * total, (slots + 1) * total), bf16),
            scratch((rows * total, 2 * LANES), bf16),
        ],
        targets, last, diagonal_partner, unit, *made, *hots)
    got = lax.all_to_all(parts, ("row", "col"), 0, 0, tiled=True)
    return call(
        functools.partial(sum_kernel, ncol, nrow), array((rows // ncol, LANES), f32), [VMEM], [], got)


def solution(mesh):
    placed = (P("row", "col", None, None), P("row", None), P("row"), P("row", None), P("row", None))

    return jax.shard_map(on_device, mesh=mesh, in_specs=placed, out_specs=P(("row", "col"), None), check_vma=False)
```
